32 devices in a mesh: region: 4 (over y, x), dom: 8 (over z, core).
Axes of the slice: x: 2, y: 2, z: 4, core: 2. Of those that a mesh axis runs over, the one named last changes fastest.
Arguments:
- theta: float32 [64, 32768], P(None, ('region', 'dom')), may hold values from -6 to 6
- salt: float32 [64, 32768], P(None, ('region', 'dom')), may hold values from -6 to 6
- ssh: float32 [32768], P(('region', 'dom')), may hold values from -6 to 6
- depth: int32 [32768], P(('region', 'dom')), may hold values from 0 to 64, as said below
- neighbors: int32 [6, 32768], P(None, ('region', 'dom')), may hold values from 0 to 4095, as said below
- send_list: int32 [16384], P(('region', 'dom')), may hold values from 0 to 1023, as said below
- weights: float32 [6, 32768], P(None, ('region', 'dom')), may hold values from 0.01 to 0.15
- kappa: float32 [63, 32768], P(None, ('region', 'dom')), may hold values from 0.05 to 5
Outputs:
- theta_next: float32 [64, 32768], P(None, ('region', 'dom'))
- salt_next: float32 [64, 32768], P(None, ('region', 'dom'))
- ssh_next: float32 [32768], P(('region', 'dom'))
The draws below stay inside these ranges and needn't reach their ends.
Inputs may be any that keep to these rules, and one draw needn't show every extreme that they name: `neighbors`: entries index a partition's extended list: 0 to 1023 the rim from the partition before, 1024 to 2047 its own cells, then 1024 cells of the partition after, then 512 cells from the region group below and 512 from the one above. A neighbour lies at most 1024 positions away along the partition's ordering unless it is a region boundary cell. `send_list`: each partition's 512 entries are distinct local positions of its own cells. `depth`: the share of land cells differs from partition to partition.
All inputs are finite; a program needn't handle non-finite values.
Results may differ from the reference program's by a relative error of at most 0.0003.
Values sent between devices are 32-bit elements; how exact they have to be, the bound alone decides.
No kernel may reach another device: no remote copies, remote signals or barrier semaphores. Data moves between devices by JAX's collectives and lax.ppermute only.
A program may use at most 128 MiB of HBM per device.

```python
import math
import jax
import jax.numpy as jnp
from jax import lax

LEV = 64
CELLS = 1024
HALO = 1024
RSEND = 512
SUB = 4
NCELLS = 32768
NSEND = 16384
N_REGION = 4
N_DOM = 8


def draw_neighbors(key, part):
    position = jnp.arange(NCELLS, dtype=jnp.int32) % CELLS
    index_rows = []
    for slot_index in range(6):
        first_key, second_key = jax.random.split(jax.random.fold_in(key, 11 + slot_index))
        magnitude = jax.random.randint(first_key, (NCELLS,), 1, HALO + 1)
        direction = jax.random.randint(second_key, (NCELLS,), 0, 2) * 2 - 1
        index_rows.append(position + direction * magnitude + HALO)
    link_key, slot_key = jax.random.split(jax.random.fold_in(key, 97))
    region_link = jax.random.randint(link_key, (NCELLS,), 0, 4) == 0
    region_slot = jax.random.randint(slot_key, (NCELLS,), 0, 2 * RSEND)
    index_rows[5] = jnp.where(region_link, CELLS + 2 * HALO + region_slot, index_rows[5])
    index_rows[0] = jnp.where(position == 0, 0, index_rows[0])
    index_rows[5] = jnp.where(position == CELLS - 1, CELLS + 2 * HALO + 2 * RSEND - 1, index_rows[5])
    return jnp.stack(index_rows).astype(jnp.int32)


def draw_send_list(key, part):
    device_count = NSEND // RSEND

    def one_device(device_index):
        interior = jax.random.permutation(jax.random.fold_in(key, 2 * device_index + 1), CELLS - 2)[:RSEND - 2] + 1
        chosen = jnp.concatenate([jnp.array([0, CELLS - 1], dtype=jnp.int32), interior.astype(jnp.int32)])
        return jax.random.permutation(jax.random.fold_in(key, 2 * device_index + 2), chosen)
    lists = jax.vmap(one_device)(jnp.arange(device_count, dtype=jnp.int32))
    return lists.reshape(NSEND).astype(jnp.int32)


def draw_depth(key, part):
    device_count = NCELLS // CELLS
    first_key, second_key, third_key = jax.random.split(jax.random.fold_in(key, 5), 3)
    land_device = jax.random.randint(first_key, (device_count,), 0, 4)
    land_share = jnp.repeat(land_device, CELLS, total_repeat_length=NCELLS)
    quarter_draw = jax.random.randint(second_key, (NCELLS,), 0, 4)
    level_draw = jax.random.randint(third_key, (NCELLS,), 1, LEV + 1)
    result = jnp.where(quarter_draw < land_share, 0, level_draw)
    position = jnp.arange(NCELLS, dtype=jnp.int32) % CELLS
    result = jnp.where(position == 0, 0, jnp.where(position == 1, LEV, result))
    return result.astype(jnp.int32)


def shard_levels(stream_key, dims, pieces, smallest, high):
    def one(dim, blocks):
        steps = jax.random.uniform(jax.random.fold_in(jax.random.fold_in(stream_key, 6), dim), (blocks,), jnp.float32, smallest / len(pieces), high / len(pieces))
        return jnp.repeat(jnp.exp(steps), dims[dim] // blocks).reshape((-1,) + (1,) * (len(dims) - dim - 1))

    loudness = one(*pieces[0])
    for cut in pieces[1:]:
        loudness = loudness * one(*cut)
    return loudness


def gaussian(stream_key, dims, deviation, limit, cuts=(), kind=jnp.bfloat16):
    gain = shard_levels(stream_key, dims, cuts, -0.22, 0.18) if cuts else 1.0
    values = jax.random.normal(stream_key, dims, jnp.float32) * deviation * gain
    return jnp.minimum(jnp.maximum(values, -limit), limit).astype(kind)


def setup_inputs(seed: int = 0) -> dict:
    keys = jax.random.split(jax.random.key(seed), 9)
    theta = gaussian(keys[0], (LEV, NCELLS), 1.0, 6.0, ((1, 32),), jnp.float32)
    salt = gaussian(keys[1], (LEV, NCELLS), 1.0, 6.0, ((1, 32),), jnp.float32)
    ssh = gaussian(keys[2], (NCELLS,), 1.0, 6.0, ((0, 32),), jnp.float32)
    depth = draw_depth(jax.random.fold_in(keys[8], 71), 0)
    neighbors = draw_neighbors(jax.random.fold_in(keys[8], 71), 0)
    send_list = draw_send_list(jax.random.fold_in(keys[8], 71), 0)
    weights = jnp.clip(jnp.exp(math.log(0.15) - 2.7080503 * jax.random.uniform(keys[6], (6, NCELLS), jnp.float32) ** shard_levels(keys[6], (6, NCELLS), ((1, 32),), -0.2, 0.2)), 0.01, 0.15)
    kappa = jnp.clip(jnp.exp(math.log(5.0) - 4.6051702 * jax.random.uniform(keys[7], (LEV - 1, NCELLS), jnp.float32) ** shard_levels(keys[7], (LEV - 1, NCELLS), ((1, 32),), -0.2, 0.2)), 0.05, 5.0)
    return dict(theta=theta, salt=salt, ssh=ssh, depth=depth, neighbors=neighbors, send_list=send_list, weights=weights, kappa=kappa)


def extended_block(block_of, send_list, device_index):
    region_index = device_index // N_DOM
    dom_index = device_index % N_DOM
    own_block = block_of(device_index)
    left_rim = block_of(jnp.maximum(device_index - 1, 0))[:, CELLS - HALO:] * (dom_index > 0).astype(own_block.dtype)
    right_rim = block_of(jnp.minimum(device_index + 1, N_REGION * N_DOM - 1))[:, :HALO] * (dom_index < N_DOM - 1).astype(own_block.dtype)
    below_index = (region_index + N_REGION - 1) % N_REGION * N_DOM + dom_index
    above_index = (region_index + 1) % N_REGION * N_DOM + dom_index

    def picked(source_index):
        positions = lax.dynamic_slice_in_dim(send_list, source_index * RSEND, RSEND, 0)
        return jnp.take(block_of(source_index), positions, axis=1)
    return jnp.concatenate([left_rim, own_block, right_rim, picked(below_index), picked(above_index)], 1)

def column_solve(rhs, coupling):
    levels = rhs.shape[1]
    ratios = []
    scaled = []
    for level_index in range(levels):
        if level_index > 0:
            below_coupling = coupling[level_index - 1]
        else:
            below_coupling = jnp.zeros_like(coupling[0])
        if level_index < levels - 1:
            above_coupling = coupling[level_index]
        else:
            above_coupling = jnp.zeros_like(coupling[0])
        diagonal = 1.0 + below_coupling + above_coupling
        if level_index > 0:
            pivot_value = diagonal - below_coupling * ratios[-1]
            solved_value = (rhs[:, level_index] + below_coupling * scaled[-1]) / pivot_value
        else:
            pivot_value = diagonal
            solved_value = rhs[:, 0] / pivot_value
        ratios.append(above_coupling / pivot_value)
        scaled.append(solved_value)
    column_value = scaled[-1]
    results = [column_value]
    for level_index in range(levels - 2, -1, -1):
        column_value = scaled[level_index] + ratios[level_index] * column_value
        results.append(column_value)
    return jnp.stack(results[::-1], 1)

def reference(theta, salt, ssh, depth, neighbors, send_list, weights, kappa):
    devices = N_REGION * N_DOM
    device_ids = jnp.arange(devices, dtype=jnp.int32)
    level_col = jnp.arange(LEV, dtype=jnp.int32)[:, None].astype(theta.dtype)

    def device_slab(array, device_index):
        return lax.dynamic_slice_in_dim(array, device_index * CELLS, CELLS, array.ndim - 1)

    def column_block(device_index):
        return jnp.concatenate([device_slab(theta, device_index), device_slab(salt, device_index), device_slab(depth, device_index).astype(theta.dtype)[None]], 0)

    def tracer_device(device_index):
        extended = extended_block(column_block, send_list, device_index)
        own_block = column_block(device_index)
        tracers = own_block[:2 * LEV]
        own_mask = (level_col < own_block[2 * LEV][None, :]).astype(theta.dtype)
        both_masks = jnp.concatenate([own_mask, own_mask], 0)
        local_neighbors = device_slab(neighbors, device_index)
        local_weights = device_slab(weights, device_index)
        accumulated = jnp.zeros_like(tracers)
        for slot_index in range(6):
            beside = jnp.take(extended, local_neighbors[slot_index], axis=1)
            beside_mask = (level_col < beside[2 * LEV][None, :]).astype(theta.dtype)
            beside_masks = jnp.concatenate([beside_mask, beside_mask], 0)
            accumulated = accumulated + local_weights[slot_index] * beside_masks * (beside[:2 * LEV] - tracers)
        stepped = tracers + both_masks * accumulated
        coupling = device_slab(kappa, device_index) * own_mask[:-1] * own_mask[1:]
        solved = column_solve(stepped.reshape(2, LEV, CELLS), coupling)
        forcing = lax.optimization_barrier(jnp.sum(own_mask * (0.2 * tracers[:LEV] - 0.15 * tracers[LEV:]), axis=0)) / math.sqrt(LEV)
        return (solved, forcing)
    solved_all, forcing_all = lax.map(tracer_device, device_ids)
    theta_next = jnp.transpose(solved_all[:, 0], (1, 0, 2)).reshape(LEV, NCELLS)
    salt_next = jnp.transpose(solved_all[:, 1], (1, 0, 2)).reshape(LEV, NCELLS)
    forcing = forcing_all.reshape(NCELLS)
    surface = ssh
    for cycle_index in range(SUB):

        def surface_device(device_index, surface=surface):

            def block_of(source_index):
                return device_slab(surface[None], source_index)
            extended = extended_block(block_of, send_list, device_index)[0]
            own_surface = device_slab(surface, device_index)
            local_neighbors = device_slab(neighbors, device_index)
            local_weights = device_slab(weights, device_index)
            tendency = jnp.zeros_like(own_surface)
            for slot_index in range(6):
                beside = jnp.take(extended, local_neighbors[slot_index], axis=0)
                tendency = tendency + local_weights[slot_index] * (beside - own_surface)
            return own_surface + tendency + 0.25 * device_slab(forcing, device_index)
        surface = lax.map(surface_device, device_ids).reshape(NCELLS)
    return (theta_next, salt_next, surface)
```

```python
import functools
import math

import jax
import jax.numpy as jnp
from jax import lax
from jax.experimental import pallas as pl
from jax.experimental.pallas import tpu as pltpu
from jax.sharding import PartitionSpec as P

AXES = ("region", "dom")
LANES = 128
TILE = 256
ROW_DEPTH = 128
ROW_INDEX = 129
ROW_WEIGHT = 135
ROW_FORCING = 141
ROW_SURFACE = 142
ROWS = 144
SMALL = 16


def lane_gather(source, lane):
    return jnp.take_along_axis(source, lane, axis=1, mode="promise_in_bounds")


def pick_block(source_rows, positions, blocks):
    lane = positions & (LANES - 1)
    block = positions >> 7
    result = lane_gather(source_rows(0), lane)
    for b in range(1, blocks):
        result = jnp.where(block == b, lane_gather(source_rows(b), lane), result)
    return result


def prepare_kernel(theta, salt, depth8, ssh8, neighbors, weights, send4, message, picked, payload):
    levels, cells = theta.shape
    blocks = cells // LANES
    message[0:levels, :] = theta[...]
    message[levels : 2 * levels, :] = salt[...]
    message[ROW_INDEX : ROW_INDEX + 6, :] = neighbors[...].astype(jnp.float32)
    message[ROW_WEIGHT : ROW_WEIGHT + 6, :] = weights[...]
    message[ROWS - 1 : ROWS, :] = jnp.zeros((1, cells), jnp.float32)
    level = lax.broadcasted_iota(jnp.int32, (levels, LANES), 0)
    for b in range(blocks):
        cols = slice(b * LANES, (b + 1) * LANES)
        depth_row = depth8[b : b + 1, :]
        message[ROW_DEPTH : ROW_DEPTH + 1, cols] = depth_row.astype(jnp.float32)
        message[ROW_SURFACE : ROW_SURFACE + 1, cols] = ssh8[b : b + 1, :]
        term = 0.2 * theta[:, cols] - 0.15 * salt[:, cols]
        total = jnp.sum(jnp.where(level < depth_row, term, 0.0), axis=0, keepdims=True)
        message[ROW_FORCING : ROW_FORCING + 1, cols] = total / math.sqrt(levels)
    send_blocks = send4.shape[0]
    for t in range(send_blocks):
        positions = jnp.broadcast_to(send4[t : t + 1, :], (8, LANES))
        cols = slice(t * LANES, (t + 1) * LANES)
        for r in range(ROWS // 8):
            rows = slice(8 * r, 8 * r + 8)
            picked[rows, cols] = pick_block(
                lambda b: message[rows, b * LANES : (b + 1) * LANES], positions, blocks
            )
    tail = jnp.concatenate(
        [
            picked[ROW_SURFACE : ROW_SURFACE + 1, t * LANES : (t + 1) * LANES]
            for t in range(send_blocks)
        ],
        axis=0,
    )
    head = ssh8[...]

    def send(i, carry):
        payload[i, 0:blocks, :] = head
        payload[i, blocks : blocks + send_blocks, :] = tail
        return carry

    lax.fori_loop(0, payload.shape[0], send, 0)


def banded_step(ext, stat, own, sub):
    total = 0.25 * stat[8 * 13 : 8 * 14, :]
    for e in range(6):
        index = stat[8 * (1 + e) : 8 * (2 + e), :].astype(jnp.int32)
        weight = stat[8 * (7 + e) : 8 * (8 + e), :]
        lane = index & (LANES - 1)
        block = index >> 7
        key = jnp.where(block >= 24, block, block - sub)
        gathered = lane_gather(ext[0:8, :], lane)
        for d in range(1, 17):
            gathered = jnp.where(key == d, lane_gather(ext[d : d + 8, :], lane), gathered)
        for b in range(24, 32):
            row = jnp.broadcast_to(ext[b : b + 1, :], (8, LANES))
            gathered = jnp.where(key == b, lane_gather(row, lane), gathered)
        total = total + weight * (gathered - own)
    return own + total


def listed_step(ext, stat, own):
    total = 0.25 * stat[8 * 13 : 8 * 14, :]
    for e in range(6):
        index = stat[8 * (1 + e) : 8 * (2 + e), :].astype(jnp.int32)
        weight = stat[8 * (7 + e) : 8 * (8 + e), :]
        gathered = pick_block(lambda b: ext[b], index, 32)
        total = total + weight * (gathered - own)
    return own + total


def surface_kernel(
    place, heights, own_small, swap_in, swap_out, below, above, send4, out,
    stat_own, stat_left, stat_right, stat_list, ext_own, ext_left, ext_right, ext_list, *, last
):
    blocks = own_small.shape[1] // LANES
    half = below.shape[1] // LANES
    odd = place[12]
    sub = lax.broadcasted_iota(jnp.int32, (8, LANES), 0)
    for b in range(blocks):
        cols = slice(b * LANES, (b + 1) * LANES)
        rows = pl.ds(b, SMALL, stride=8)
        first = swap_in[:, cols]
        second = swap_out[:, cols]
        stat_own[rows, :] = own_small[:, cols]
        stat_left[rows, :] = jnp.where(odd == 1, first, second)
        stat_right[rows, :] = jnp.where(odd == 1, second, first)
    for b in range(half):
        cols = slice(b * LANES, (b + 1) * LANES)
        stat_list[pl.ds(b, SMALL, stride=8), :] = below[:, cols]
        stat_list[pl.ds(half + b, SMALL, stride=8), :] = above[:, cols]

    def full(n, side):
        value = heights[place[n], 0:8, :]
        if side is None:
            return value
        return jnp.where(place[13 + side] == 1, value, 0.0)

    def listed(n):
        return heights[place[n], 8:12, :]

    own = full(0, None)
    left2, left, right, right2 = full(1, 0), full(2, 1), full(3, 2), full(4, 3)
    ext_own[0:8, :] = left
    ext_own[8:16, :] = own
    ext_own[16:24, :] = right
    ext_own[24:28, :] = listed(6)
    ext_own[28:32, :] = listed(9)
    ext_left[0:8, :] = left2
    ext_left[8:16, :] = left
    ext_left[16:24, :] = own
    ext_left[24:28, :] = listed(5)
    ext_left[28:32, :] = listed(8)
    ext_right[0:8, :] = own
    ext_right[8:16, :] = right
    ext_right[16:24, :] = right2
    ext_right[24:28, :] = listed(7)
    ext_right[28:32, :] = listed(10)
    low = sub < 4
    below_ext = [full(5, 1), full(6, None), full(7, 2)]
    above_ext = [full(8, 1), full(9, None), full(10, 2)]
    for part in range(3):
        for b in range(8):
            ext_list[8 * part + b] = jnp.where(
                low,
                jnp.broadcast_to(below_ext[part][b : b + 1, :], (8, LANES)),
                jnp.broadcast_to(above_ext[part][b : b + 1, :], (8, LANES)),
            )
    own_listed = listed(0)
    tails = [(listed(11), own_listed), (own_listed, listed(17))]
    for part in range(2):
        for b in range(4):
            ext_list[24 + 4 * part + b] = jnp.where(
                low,
                jnp.broadcast_to(tails[part][0][b : b + 1, :], (8, LANES)),
                jnp.broadcast_to(tails[part][1][b : b + 1, :], (8, LANES)),
            )
    own_list = jnp.concatenate([listed(6), listed(9)], axis=0)
    new_own = banded_step(ext_own, stat_own, own, sub)
    new_left = banded_step(ext_left, stat_left, left, sub)
    new_right = banded_step(ext_right, stat_right, right, sub)
    new_list = listed_step(ext_list, stat_list, own_list)
    ext_own[0:8, :] = jnp.where(place[14] == 1, new_left, 0.0)
    ext_own[8:16, :] = new_own
    ext_own[16:24, :] = jnp.where(place[15] == 1, new_right, 0.0)
    ext_own[24:32, :] = new_list
    final = banded_step(ext_own, stat_own, new_own, sub)
    if last:
        out[...] = final
        return
    ext_left[0:8, :] = final
    positions = jnp.concatenate([send4[...], send4[...]], axis=0)
    tail = pick_block(
        lambda b: jnp.broadcast_to(ext_left[b : b + 1, :], (8, LANES)), positions, blocks
    )

    def send(i, carry):
        out[i, 0:8, :] = final
        out[i, 8:12, :] = tail[0:4, :]
        return carry

    lax.fori_loop(0, out.shape[0], send, 0)


def pivot_kernel(kappa, depth8, ratio, lower, inverse, kap):
    levels = inverse.shape[0] // 8
    cells = kappa.shape[1]
    for b in range(cells // LANES):
        cols = slice(b * LANES, (b + 1) * LANES)
        kap[pl.ds(b, levels - 1, stride=8), :] = kappa[:, cols]
    depth = depth8[...]
    before = jnp.zeros((8, LANES), jnp.float32)
    last_ratio = before
    for k in range(levels):
        rows = slice(8 * k, 8 * k + 8)
        if k < levels - 1:
            after = jnp.where(depth > k + 1, kap[rows, :], 0.0)
        else:
            after = jnp.zeros((8, LANES), jnp.float32)
        pivot = 1.0 + before + after - before * last_ratio
        inv = 1.0 / pivot
        last_ratio = after * inv
        inverse[rows, :] = inv
        lower[rows, :] = before * inv
        ratio[rows, :] = last_ratio
        before = after


def tracer_kernel(
    place, own, swap_in, swap_out, below, above, ratio, lower, inverse, theta_next, salt_next,
    rows_ext, merged, star
):
    levels, cells = theta_next.shape
    listed = below.shape[1]
    level = lax.broadcasted_iota(jnp.int32, (levels, LANES), 0).astype(jnp.float32)
    ext_width = 3 * cells + 2 * listed

    def stage(source, width, offset):
        for b in range(width // LANES):
            cols = slice(b * LANES, (b + 1) * LANES)
            target = pl.ds(offset + b * LANES, LANES)
            wet = (level < source[ROW_DEPTH : ROW_DEPTH + 1, cols]).astype(jnp.float32)
            first = source[0:levels, cols] * wet
            second = source[levels : 2 * levels, cols] * wet
            high0 = first.astype(jnp.bfloat16)
            high1 = second.astype(jnp.bfloat16)
            rows_ext[0:levels, target] = (first - high0.astype(jnp.float32)).astype(jnp.bfloat16)
            rows_ext[levels : 2 * levels, target] = (
                second - high1.astype(jnp.float32)
            ).astype(jnp.bfloat16)
            rows_ext[2 * levels : 3 * levels, target] = high0
            rows_ext[3 * levels : 4 * levels, target] = high1
            rows_ext[4 * levels : 5 * levels, target] = wet.astype(jnp.bfloat16)

    inner = pl.multiple_of(place[12] * 0 + jnp.where(place[12] == 1, 0, 2 * cells), LANES)
    outer = pl.multiple_of(jnp.where(place[12] == 1, 2 * cells, 0), LANES)
    stage(own, cells, cells)
    stage(swap_in, cells, inner)
    stage(swap_out, cells, outer)
    stage(below, listed, 3 * cells)
    stage(above, listed, 3 * cells + listed)

    index = [own[ROW_INDEX + e : ROW_INDEX + e + 1, :].astype(jnp.int32) for e in range(6)]
    weight = [own[ROW_WEIGHT + e : ROW_WEIGHT + e + 1, :] for e in range(6)]
    for e in range(5, 0, -1):
        taken = index[e] < 0
        for f in range(e):
            same = jnp.logical_and(index[e] == index[f], jnp.logical_not(taken))
            weight[f] = weight[f] + jnp.where(same, weight[e], 0.0)
            taken = jnp.logical_or(taken, same)
        index[e] = jnp.where(taken, -1, index[e])
    for e in range(6):
        merged[e : e + 1, :] = index[e].astype(jnp.float32)
        merged[8 + e : 9 + e, :] = weight[e]
    line = lax.broadcasted_iota(jnp.int32, (TILE, TILE), 0).astype(jnp.float32).astype(jnp.bfloat16)
    band = (TILE + 2 * cells) // TILE
    region = 2 * listed // TILE

    def block(t, carry):
        start = pl.multiple_of(t * TILE, TILE)
        idx = [merged[e : e + 1, pl.ds(start, TILE)].astype(jnp.int32) for e in range(6)]
        wts = [merged[8 + e : 9 + e, pl.ds(start, TILE)] for e in range(6)]
        highs = [w.astype(jnp.bfloat16) for w in wts]
        lows = [(w - h.astype(jnp.float32)).astype(jnp.bfloat16) for w, h in zip(wts, highs)]
        total = jnp.zeros((5 * levels, TILE), jnp.float32)
        extra = jnp.zeros((3 * levels, TILE), jnp.float32)
        for j in range(band + region):
            if j < band:
                base = start + j * TILE
            else:
                base = 3 * cells + (j - band) * TILE
            base = pl.multiple_of(base, TILE)
            high = jnp.zeros((TILE, TILE), jnp.bfloat16)
            low = jnp.zeros((TILE, TILE), jnp.bfloat16)
            for e in range(6):
                local = idx[e] - base
                local = jnp.where(jnp.logical_and(local >= 0, local < TILE), local, -1)
                local = local.astype(jnp.float32).astype(jnp.bfloat16)
                hit = line == local
                high = jnp.where(hit, highs[e], high)
                low = jnp.where(hit, lows[e], low)
            total = total + jnp.dot(
                rows_ext[:, pl.ds(base, TILE)], high, preferred_element_type=jnp.float32
            )
            extra = extra + jnp.dot(
                rows_ext[2 * levels :, pl.ds(base, TILE)], low, preferred_element_type=jnp.float32
            )
        wet_sum = total[4 * levels :] + extra[2 * levels :]
        for b in range(TILE // LANES):
            cols = slice(b * LANES, (b + 1) * LANES)
            here = pl.ds(start + b * LANES, LANES)
            wet = level < own[ROW_DEPTH : ROW_DEPTH + 1, here]
            for c in range(2):
                value = own[c * levels : (c + 1) * levels, here]
                acc = (
                    total[c * levels : (c + 1) * levels, cols]
                    + total[(2 + c) * levels : (3 + c) * levels, cols]
                    + extra[c * levels : (c + 1) * levels, cols]
                )
                stepped = value + jnp.where(wet, acc - value * wet_sum[:, cols], 0.0)
                star[c, pl.ds(t * (TILE // LANES) + b, levels, stride=8), :] = stepped
        return carry

    lax.fori_loop(0, cells // TILE, block, 0)
    for c in range(2):
        star[c] = star[c] * inverse[...]
    before = [star[0, 0:8, :], star[1, 0:8, :]]
    for k in range(1, levels):
        rows = slice(8 * k, 8 * k + 8)
        factor = lower[rows, :]
        for c in range(2):
            before[c] = star[c, rows, :] + factor * before[c]
            star[c, rows, :] = before[c]
    for k in range(levels - 2, -1, -1):
        rows = slice(8 * k, 8 * k + 8)
        factor = ratio[rows, :]
        for c in range(2):
            before[c] = star[c, rows, :] + factor * before[c]
            star[c, rows, :] = before[c]
    for b in range(cells // LANES):
        cols = slice(b * LANES, (b + 1) * LANES)
        theta_next[:, cols] = star[0, pl.ds(b, levels, stride=8), :]
        salt_next[:, cols] = star[1, pl.ds(b, levels, stride=8), :]


VMEM = pl.BlockSpec(memory_space=pltpu.VMEM)
SMEM = pl.BlockSpec(memory_space=pltpu.SMEM)


def estimate(flops, size):
    return pl.CostEstimate(flops=flops, bytes_accessed=size, transcendentals=0)


def body(regions, doms, theta, salt, ssh, depth, neighbors, send_list, weights, kappa):
    levels, cells = theta.shape
    listed = send_list.shape[0]
    devices = regions * doms
    f32 = jnp.float32
    depth8 = depth.reshape(cells // LANES, LANES)
    ssh8 = ssh.reshape(cells // LANES, LANES)
    send4 = send_list.reshape(listed // LANES, LANES)
    r = lax.axis_index("region")
    q = lax.axis_index("dom")

    def at(dr, dq):
        return ((r + dr) % regions) * doms + jnp.clip(q + dq, 0, doms - 1)

    place = jnp.stack(
        [
            at(0, 0), at(0, -2), at(0, -1), at(0, 1), at(0, 2),
            at(-1, -1), at(-1, 0), at(-1, 1), at(1, -1), at(1, 0), at(1, 1), at(-2, 0),
            q % 2, (q >= 2), (q >= 1), (q < doms - 1), (q < doms - 2), at(2, 0),
        ]
    ).astype(jnp.int32)
    payload_shape = jax.ShapeDtypeStruct((devices, 12, LANES), f32)
    message, picked, payload = pl.pallas_call(
        prepare_kernel,
        out_shape=(
            jax.ShapeDtypeStruct((ROWS, cells), f32),
            jax.ShapeDtypeStruct((ROWS, listed), f32),
            payload_shape,
        ),
        in_specs=[VMEM] * 7,
        out_specs=(VMEM,) * 3,
        name="prepare",
    )(theta, salt, depth8, ssh8, neighbors, weights, send4)

    def device(i, j):
        return (i % regions) * doms + j

    inner = [(device(i, j), device(i, j ^ 1)) for i in range(regions) for j in range(doms)]
    outer = [
        (device(i, j), device(i, j + 1 if j % 2 else j - 1))
        for i in range(regions)
        for j in range(1, doms - 1)
    ]
    upward = [(device(i, j), device(i + 1, j)) for i in range(regions) for j in range(doms)]
    downward = [(target, source) for source, target in upward]
    below = lax.ppermute(picked, AXES, upward)
    above = lax.ppermute(picked, AXES, downward)
    swap_in = lax.ppermute(message, AXES, inner)
    swap_out = lax.ppermute(message, AXES, outer)
    heights = lax.all_to_all(payload, AXES, 0, 0)
    ratio, lower, inverse = pl.pallas_call(
        pivot_kernel,
        out_shape=(jax.ShapeDtypeStruct((8 * levels, LANES), f32),) * 3,
        in_specs=[VMEM] * 2,
        out_specs=(VMEM,) * 3,
        scratch_shapes=[pltpu.VMEM((8 * levels, LANES), f32)],
        cost_estimate=estimate(1000000, 1000000),
        name="pivots",
    )(kappa, depth8)
    small = pl.BlockSpec((SMALL, cells), lambda *_: (ROW_DEPTH // SMALL, 0))
    small_listed = pl.BlockSpec((SMALL, listed), lambda *_: (ROW_DEPTH // SMALL, 0))

    def subcycles(values, last):
        return pl.pallas_call(
            functools.partial(surface_kernel, last=last),
            out_shape=jax.ShapeDtypeStruct((8, LANES), f32) if last else payload_shape,
            grid=(1,),
            in_specs=[SMEM, VMEM, small, small, small, small_listed, small_listed, VMEM],
            out_specs=VMEM,
            scratch_shapes=[pltpu.VMEM((8 * SMALL, LANES), f32)] * 4
            + [pltpu.VMEM((32, LANES), f32)] * 3
            + [pltpu.VMEM((32, 8, LANES), f32)],
            cost_estimate=estimate(2000000, 1000000),
            name="surface_last" if last else "surface_first",
        )(place, values, message, swap_in, swap_out, picked_below, picked_above, send4)

    picked_below, picked_above = below, above
    payload2 = subcycles(heights, False)
    heights2 = lax.all_to_all(payload2, AXES, 0, 0)
    surface = subcycles(heights2, True)
    theta_next, salt_next = pl.pallas_call(
        tracer_kernel,
        out_shape=(jax.ShapeDtypeStruct((levels, cells), f32),) * 2,
        in_specs=[SMEM] + [VMEM] * 8,
        out_specs=(VMEM,) * 2,
        scratch_shapes=[
            pltpu.VMEM((5 * levels, 3 * cells + 2 * listed), jnp.bfloat16),
            pltpu.VMEM((16, cells), f32),
            pltpu.VMEM((2, 8 * levels, LANES), f32),
        ],
        cost_estimate=estimate(4000000000, 4000000),
        compiler_params=pltpu.CompilerParams(vmem_limit_bytes=40 * 1024 * 1024),
        name="tracers",
    )(place, message, swap_in, swap_out, below, above, ratio, lower, inverse)
    return (theta_next, salt_next, surface.reshape(cells))


def solution(mesh):
    columns = P(None, AXES)
    cells = P(AXES)
    return jax.shard_map(
        functools.partial(body, mesh.shape["region"], mesh.shape["dom"]),
        mesh=mesh,
        in_specs=(columns, columns, cells, cells, columns, cells, columns, columns),
        out_specs=(columns, columns, cells),
        check_vma=False,
    )
```

```python
import functools
import math

import jax
import jax.numpy as jnp
from jax import lax
from jax.experimental import pallas as pl
from jax.experimental.pallas import tpu as pltpu
from jax.sharding import PartitionSpec as P

AXES = ("region", "dom")
LANES = 128
TILE = 256
ROW_DEPTH = 0
ROW_INDEX = 1
ROW_WEIGHT = 7
ROW_FORCING = 13
ROW_SURFACE = 14
SMALL = 16
PART_INDEX = 192
PART_WEIGHT = 200


def lane_gather(source, lane):
    return jnp.take_along_axis(source, lane, axis=1, mode="promise_in_bounds")


def pick_block(source_rows, positions, blocks):
    lane = positions & (LANES - 1)
    block = positions >> 7
    result = lane_gather(source_rows(0), lane)
    for b in range(1, blocks):
        result = jnp.where(block == b, lane_gather(source_rows(b), lane), result)
    return result


def copies(pairs, semaphores):
    started = []
    for n, (source, target) in enumerate(pairs):
        copy = pltpu.make_async_copy(source, target, semaphores.at[n])
        copy.start()
        started.append(copy)
    return started


def prepare_kernel(
    theta_in, salt_in, depth8, ssh8, neighbors, weights, send4,
    small, picked_small, picked, payload,
    theta, salt, depths, heights, nbr, wts, sends, loaded
):
    levels, cells = theta.shape
    blocks = cells // LANES
    arrivals = copies(
        [
            (send4, sends), (ssh8, heights), (depth8, depths), (neighbors, nbr), (weights, wts),
            (theta_in, theta), (salt_in, salt),
        ],
        loaded,
    )
    for copy in arrivals[:5]:
        copy.wait()
    small[ROW_INDEX : ROW_INDEX + 6, :] = nbr[...].astype(jnp.float32)
    small[ROW_WEIGHT : ROW_WEIGHT + 6, :] = wts[...]
    small[SMALL - 1 : SMALL, :] = jnp.zeros((1, cells), jnp.float32)
    level = lax.broadcasted_iota(jnp.int32, (levels, LANES), 0)
    for b in range(blocks):
        cols = slice(b * LANES, (b + 1) * LANES)
        small[ROW_DEPTH : ROW_DEPTH + 1, cols] = depths[b : b + 1, :].astype(jnp.float32)
        small[ROW_SURFACE : ROW_SURFACE + 1, cols] = heights[b : b + 1, :]
    send_blocks = sends.shape[0]

    def pick(source, target, groups, offset):
        for t in range(send_blocks):
            positions = jnp.broadcast_to(sends[t : t + 1, :], (8, LANES))
            for r in range(groups):
                rows = slice(8 * r, 8 * r + 8)
                target[offset + 8 * r : offset + 8 * r + 8, t * LANES : (t + 1) * LANES] = pick_block(
                    lambda b: source[rows, b * LANES : (b + 1) * LANES], positions, blocks
                )

    arrivals[5].wait()
    pick(theta, picked, levels // 8, 0)
    arrivals[6].wait()
    pick(salt, picked, levels // 8, levels)
    for b in range(blocks):
        cols = slice(b * LANES, (b + 1) * LANES)
        term = 0.2 * theta[:, cols] - 0.15 * salt[:, cols]
        wet = level < depths[b : b + 1, :]
        total = jnp.sum(jnp.where(wet, term, 0.0), axis=0, keepdims=True)
        small[ROW_FORCING : ROW_FORCING + 1, cols] = total / math.sqrt(levels)
    pick(small, picked_small, SMALL // 8, 0)
    tail = jnp.concatenate(
        [
            picked_small[ROW_SURFACE : ROW_SURFACE + 1, t * LANES : (t + 1) * LANES]
            for t in range(send_blocks)
        ],
        axis=0,
    )
    head = heights[...]

    def send(i, carry):
        payload[i, 0:blocks, :] = head
        payload[i, blocks : blocks + send_blocks, :] = tail
        return carry

    lax.fori_loop(0, payload.shape[0], send, 0)


def banded_step(ext, stat, own, sub):
    total = 0.25 * stat[8 * 13 : 8 * 14, :]
    for e in range(6):
        index = stat[8 * (1 + e) : 8 * (2 + e), :].astype(jnp.int32)
        weight = stat[8 * (7 + e) : 8 * (8 + e), :]
        lane = index & (LANES - 1)
        block = index >> 7
        key = jnp.where(block >= 24, block, block - sub)
        gathered = lane_gather(ext[0:8, :], lane)
        for d in range(1, 17):
            gathered = jnp.where(key == d, lane_gather(ext[d : d + 8, :], lane), gathered)
        for b in range(24, 32):
            row = jnp.broadcast_to(ext[b : b + 1, :], (8, LANES))
            gathered = jnp.where(key == b, lane_gather(row, lane), gathered)
        total = total + weight * (gathered - own)
    return own + total


def listed_step(ext, stat, own):
    total = 0.25 * stat[8 * 13 : 8 * 14, :]
    for e in range(6):
        index = stat[8 * (1 + e) : 8 * (2 + e), :].astype(jnp.int32)
        weight = stat[8 * (7 + e) : 8 * (8 + e), :]
        gathered = pick_block(lambda b: ext[b], index, 32)
        total = total + weight * (gathered - own)
    return own + total


def surface_kernel(
    place, heights, own_in, swap_in, swap_out, below, above, sends, token, out,
    stat_own, stat_left, stat_right, stat_list, ext_own, ext_left, ext_right, ext_list, *, last
):
    blocks = own_in.shape[1] // LANES
    half = below.shape[1] // LANES
    odd = place[12]
    sub = lax.broadcasted_iota(jnp.int32, (8, LANES), 0)
    for b in range(blocks):
        cols = slice(b * LANES, (b + 1) * LANES)
        rows = pl.ds(b, SMALL, stride=8)
        first = swap_in[:, cols]
        second = swap_out[:, cols]
        stat_own[rows, :] = own_in[:, cols]
        stat_left[rows, :] = jnp.where(odd == 1, first, second)
        stat_right[rows, :] = jnp.where(odd == 1, second, first)
    for b in range(half):
        cols = slice(b * LANES, (b + 1) * LANES)
        stat_list[pl.ds(b, SMALL, stride=8), :] = below[:, cols]
        stat_list[pl.ds(half + b, SMALL, stride=8), :] = above[:, cols]

    def full(n, side):
        value = heights[place[n], 0:8, :]
        if side is None:
            return value
        return jnp.where(place[13 + side] == 1, value, 0.0)

    def listed(n):
        return heights[place[n], 8:12, :]

    own = full(0, None)
    left2, left, right, right2 = full(1, 0), full(2, 1), full(3, 2), full(4, 3)
    ext_own[0:8, :] = left
    ext_own[8:16, :] = own
    ext_own[16:24, :] = right
    ext_own[24:28, :] = listed(6)
    ext_own[28:32, :] = listed(9)
    ext_left[0:8, :] = left2
    ext_left[8:16, :] = left
    ext_left[16:24, :] = own
    ext_left[24:28, :] = listed(5)
    ext_left[28:32, :] = listed(8)
    ext_right[0:8, :] = own
    ext_right[8:16, :] = right
    ext_right[16:24, :] = right2
    ext_right[24:28, :] = listed(7)
    ext_right[28:32, :] = listed(10)
    low = sub < 4
    below_ext = [full(5, 1), full(6, None), full(7, 2)]
    above_ext = [full(8, 1), full(9, None), full(10, 2)]
    for part in range(3):
        for b in range(8):
            ext_list[8 * part + b] = jnp.where(
                low,
                jnp.broadcast_to(below_ext[part][b : b + 1, :], (8, LANES)),
                jnp.broadcast_to(above_ext[part][b : b + 1, :], (8, LANES)),
            )
    own_listed = listed(0)
    tails = [(listed(11), own_listed), (own_listed, listed(17))]
    for part in range(2):
        for b in range(4):
            ext_list[24 + 4 * part + b] = jnp.where(
                low,
                jnp.broadcast_to(tails[part][0][b : b + 1, :], (8, LANES)),
                jnp.broadcast_to(tails[part][1][b : b + 1, :], (8, LANES)),
            )
    own_list = jnp.concatenate([listed(6), listed(9)], axis=0)
    new_own = banded_step(ext_own, stat_own, own, sub)
    new_left = banded_step(ext_left, stat_left, left, sub)
    new_right = banded_step(ext_right, stat_right, right, sub)
    new_list = listed_step(ext_list, stat_list, own_list)
    ext_own[0:8, :] = jnp.where(place[14] == 1, new_left, 0.0)
    ext_own[8:16, :] = new_own
    ext_own[16:24, :] = jnp.where(place[15] == 1, new_right, 0.0)
    ext_own[24:32, :] = new_list
    final = banded_step(ext_own, stat_own, new_own, sub)
    if last:
        out[...] = final
        return
    ext_left[0:8, :] = final
    positions = jnp.concatenate([sends[...], sends[...]], axis=0)
    tail = pick_block(
        lambda b: jnp.broadcast_to(ext_left[b : b + 1, :], (8, LANES)), positions, blocks
    )

    def send(i, carry):
        out[i, 0:8, :] = final
        out[i, 8:12, :] = tail[0:4, :]
        return carry

    lax.fori_loop(0, out.shape[0], send, 0)


def stage(sources, depth, target, width, offset, level):
    levels = level.shape[0]
    for b in range(width // LANES):
        cols = slice(b * LANES, (b + 1) * LANES)
        where = pl.ds(offset + b * LANES, LANES)
        wet = (level < depth[ROW_DEPTH : ROW_DEPTH + 1, cols]).astype(jnp.float32)
        for c in range(2):
            value = sources[c][:, cols] * wet
            high = value.astype(jnp.bfloat16)
            low = (value - high.astype(jnp.float32)).astype(jnp.bfloat16)
            target[c * levels : (c + 1) * levels, where] = low
            target[(2 + c) * levels : (3 + c) * levels, where] = high
        target[4 * levels : 5 * levels, where] = wet.astype(jnp.bfloat16)


def weight_tile(line, index, highs, lows, base):
    high = jnp.zeros((TILE, TILE), jnp.bfloat16)
    low = jnp.zeros((TILE, TILE), jnp.bfloat16)
    for e in range(6):
        local = index[e] - base
        local = jnp.where(jnp.logical_and(local >= 0, local < TILE), local, -1)
        local = local.astype(jnp.float32).astype(jnp.bfloat16)
        hit = line == local
        high = jnp.where(hit, highs[e], high)
        low = jnp.where(hit, lows[e], low)
    return high, low


def tile_line():
    line = lax.broadcasted_iota(jnp.int32, (TILE, TILE), 0)
    return line.astype(jnp.float32).astype(jnp.bfloat16)


def split_weights(rows, columns):
    weights = [rows[e : e + 1, columns] for e in range(6)]
    highs = [w.astype(jnp.bfloat16) for w in weights]
    lows = [(w - h.astype(jnp.float32)).astype(jnp.bfloat16) for w, h in zip(weights, highs)]
    return highs, lows


def product(rows, columns, high, low, levels):
    first = jnp.dot(rows[:, columns], high, preferred_element_type=jnp.float32)
    second = jnp.dot(rows[2 * levels :, columns], low, preferred_element_type=jnp.float32)
    return jnp.concatenate(
        [
            first[0 : 2 * levels] + first[2 * levels : 4 * levels] + second[0 : 2 * levels],
            first[4 * levels :] + second[2 * levels :],
        ],
        axis=0,
    )


def local_kernel(
    theta_in, salt_in, small, kappa_in, depth_in, pivots, part, token,
    theta, salt, kappa, depth8, kap, rows_own, loaded
):
    cells = small.shape[1]
    levels = pivots.shape[1] // 8
    arrivals = copies(
        [(depth_in, depth8), (kappa_in, kappa), (theta_in, theta), (salt_in, salt)], loaded
    )
    for copy in arrivals[:2]:
        copy.wait()
    for b in range(cells // LANES):
        cols = slice(b * LANES, (b + 1) * LANES)
        kap[pl.ds(b, levels - 1, stride=8), :] = kappa[:, cols]
    depth = depth8[...]
    before = jnp.zeros((8, LANES), jnp.float32)
    last_ratio = before
    for k in range(levels):
        rows = slice(8 * k, 8 * k + 8)
        if k < levels - 1:
            after = jnp.where(depth > k + 1, kap[rows, :], 0.0)
        else:
            after = jnp.zeros((8, LANES), jnp.float32)
        pivot = 1.0 + before + after - before * last_ratio
        inverse = 1.0 / pivot
        last_ratio = after * inverse
        pivots[0, rows, :] = last_ratio
        pivots[1, rows, :] = before * inverse
        pivots[2, rows, :] = inverse
        before = after
    index = [small[ROW_INDEX + e : ROW_INDEX + e + 1, :].astype(jnp.int32) for e in range(6)]
    weight = [small[ROW_WEIGHT + e : ROW_WEIGHT + e + 1, :] for e in range(6)]
    for e in range(5, 0, -1):
        taken = index[e] < 0
        for f in range(e):
            same = jnp.logical_and(index[e] == index[f], jnp.logical_not(taken))
            weight[f] = weight[f] + jnp.where(same, weight[e], 0.0)
            taken = jnp.logical_or(taken, same)
        index[e] = jnp.where(taken, -1, index[e])
    for e in range(6):
        part[PART_INDEX + e : PART_INDEX + e + 1, :] = index[e].astype(jnp.float32)
        part[PART_WEIGHT + e : PART_WEIGHT + e + 1, :] = weight[e]
    token[...] = depth
    level = lax.broadcasted_iota(jnp.int32, (levels, LANES), 0).astype(jnp.float32)
    for copy in arrivals[2:]:
        copy.wait()
    stage((theta, salt), small, rows_own, cells, 0, level)
    line = tile_line()

    def block(t, carry):
        here = pl.ds(pl.multiple_of(t * TILE, TILE), TILE)
        idx = [part[PART_INDEX + e : PART_INDEX + e + 1, here].astype(jnp.int32) for e in range(6)]
        highs, lows = split_weights(part.at[pl.ds(PART_WEIGHT, 8), :], here)
        total = jnp.zeros((3 * levels, TILE), jnp.float32)
        for j in range(cells // TILE):
            high, low = weight_tile(line, idx, highs, lows, cells + j * TILE)
            columns = slice(j * TILE, (j + 1) * TILE)
            total = total + product(rows_own, columns, high, low, levels)
        part[0 : 3 * levels, here] = total
        return carry

    lax.fori_loop(0, cells // TILE, block, 0)


def tracer_kernel(
    place, theta_in, salt_in, small, theta_inner, salt_inner, small_inner, theta_outer, salt_outer,
    small_outer, below, small_below, above, small_above, pivots, part, theta_out, salt_out,
    own, rows_ext, star, result, loaded, stored
):
    levels, cells = theta_out.shape
    listed = below.shape[1]
    arrivals = copies([(theta_in, own.at[0]), (salt_in, own.at[1])], loaded)
    level = lax.broadcasted_iota(jnp.int32, (levels, LANES), 0).astype(jnp.float32)
    odd = place[12] == 1
    inner = pl.multiple_of(jnp.where(odd, 0, cells), LANES)
    outer = pl.multiple_of(jnp.where(odd, cells, 0), LANES)
    stage((theta_inner, salt_inner), small_inner, rows_ext, cells, inner, level)
    stage((theta_outer, salt_outer), small_outer, rows_ext, cells, outer, level)

    def halves(picked):
        return picked.at[pl.ds(0, levels), :], picked.at[pl.ds(levels, levels), :]

    stage(halves(below), small_below, rows_ext, listed, 2 * cells, level)
    stage(halves(above), small_above, rows_ext, listed, 2 * cells + listed, level)
    for copy in arrivals:
        copy.wait()
    line = tile_line()
    band = (TILE + cells) // TILE
    region = 2 * listed // TILE

    def block(t, carry):
        start = pl.multiple_of(t * TILE, TILE)
        here = pl.ds(start, TILE)
        idx = []
        for e in range(6):
            value = part[PART_INDEX + e : PART_INDEX + e + 1, here].astype(jnp.int32)
            outside = jnp.where(value >= 2 * cells, value - cells, -1)
            idx.append(jnp.where(value < cells, value, outside))
        highs, lows = split_weights(part.at[pl.ds(PART_WEIGHT, 8), :], here)
        total = part[0 : 3 * levels, here]
        for j in range(band + region):
            base = start + j * TILE if j < band else 2 * cells + (j - band) * TILE
            base = pl.multiple_of(base, TILE)
            high, low = weight_tile(line, idx, highs, lows, base)
            total = total + product(rows_ext, pl.ds(base, TILE), high, low, levels)
        for b in range(TILE // LANES):
            cols = slice(b * LANES, (b + 1) * LANES)
            sub = pl.ds(start + b * LANES, LANES)
            wet = level < small[ROW_DEPTH : ROW_DEPTH + 1, sub]
            for c in range(2):
                value = own[c, :, sub]
                change = total[c * levels : (c + 1) * levels, cols] - value * total[2 * levels :, cols]
                stepped = value + jnp.where(wet, change, 0.0)
                star[c, pl.ds(t * (TILE // LANES) + b, levels, stride=8), :] = stepped
        return carry

    lax.fori_loop(0, cells // TILE, block, 0)
    for c in range(2):
        star[c] = star[c] * pivots[2]
    before = [star[0, 0:8, :], star[1, 0:8, :]]
    for k in range(1, levels):
        rows = slice(8 * k, 8 * k + 8)
        factor = pivots[1, rows, :]
        for c in range(2):
            before[c] = star[c, rows, :] + factor * before[c]
            star[c, rows, :] = before[c]
    for k in range(levels - 2, -1, -1):
        rows = slice(8 * k, 8 * k + 8)
        factor = pivots[0, rows, :]
        for c in range(2):
            before[c] = star[c, rows, :] + factor * before[c]
            star[c, rows, :] = before[c]
    departures = []
    for c, out in enumerate((theta_out, salt_out)):
        for b in range(cells // LANES):
            cols = slice(b * LANES, (b + 1) * LANES)
            result[c, :, cols] = star[c, pl.ds(b, levels, stride=8), :]
            if b % 4 == 3:
                done = pl.ds((b - 3) * LANES, 4 * LANES)
                departures += copies(
                    [(result.at[c, :, done], out.at[:, done])],
                    stored.at[pl.ds(2 * c + b // 4, 1)],
                )
    for copy in departures:
        copy.wait()


HBM = pl.BlockSpec(memory_space=pltpu.HBM)
VMEM = pl.BlockSpec(memory_space=pltpu.VMEM)
SMEM = pl.BlockSpec(memory_space=pltpu.SMEM)


def grant(mebibytes):
    return pltpu.CompilerParams(vmem_limit_bytes=mebibytes * 1024 * 1024)


def estimate(flops, size):
    return pl.CostEstimate(flops=flops, bytes_accessed=size, transcendentals=0)


def body(regions, doms, theta, salt, ssh, depth, neighbors, send_list, weights, kappa):
    levels, cells = theta.shape
    listed = send_list.shape[0]
    devices = regions * doms
    f32 = jnp.float32
    depth8 = depth.reshape(cells // LANES, LANES)
    ssh8 = ssh.reshape(cells // LANES, LANES)
    send4 = send_list.reshape(listed // LANES, LANES)
    r = lax.axis_index("region")
    q = lax.axis_index("dom")

    def at(dr, dq):
        return ((r + dr) % regions) * doms + jnp.clip(q + dq, 0, doms - 1)

    place = jnp.stack(
        [
            at(0, 0), at(0, -2), at(0, -1), at(0, 1), at(0, 2),
            at(-1, -1), at(-1, 0), at(-1, 1), at(1, -1), at(1, 0), at(1, 1), at(-2, 0),
            q % 2, (q >= 2), (q >= 1), (q < doms - 1), (q < doms - 2), at(2, 0),
        ]
    ).astype(jnp.int32)
    def vmem(*shape, dtype=f32):
        return pltpu.VMEM(shape, dtype)

    def semaphores(count):
        return pltpu.SemaphoreType.DMA((count,))

    payload_shape = jax.ShapeDtypeStruct((devices, 12, LANES), f32)

    def hbm(*arrays):
        return [pltpu.with_memory_space_constraint(array, pltpu.HBM) for array in arrays]

    small, picked_small, picked, payload = pl.pallas_call(
        prepare_kernel,
        out_shape=(
            jax.ShapeDtypeStruct((SMALL, cells), f32),
            jax.ShapeDtypeStruct((SMALL, listed), f32),
            jax.ShapeDtypeStruct((2 * levels, listed), f32),
            payload_shape,
        ),
        in_specs=[HBM] * 7,
        out_specs=(VMEM,) * 4,
        scratch_shapes=[
            vmem(levels, cells), vmem(levels, cells),
            vmem(8, LANES, dtype=jnp.int32), vmem(8, LANES), vmem(6, cells, dtype=jnp.int32),
            vmem(6, cells), vmem(listed // LANES, LANES, dtype=jnp.int32), semaphores(7),
        ],
        compiler_params=grant(8),
        name="prepare",
    )(*hbm(theta, salt, depth8, ssh8, neighbors, weights, send4))

    def device(i, j):
        return (i % regions) * doms + j

    inner = [(device(i, j), device(i, j ^ 1)) for i in range(regions) for j in range(doms)]
    outer = [
        (device(i, j), device(i, j + 1 if j % 2 else j - 1))
        for i in range(regions)
        for j in range(1, doms - 1)
    ]
    upward = [(device(i, j), device(i + 1, j)) for i in range(regions) for j in range(doms)]
    downward = [(target, source) for source, target in upward]
    below = lax.ppermute(picked, AXES, upward)
    above = lax.ppermute(picked, AXES, downward)
    small_below = lax.ppermute(picked_small, AXES, upward)
    small_above = lax.ppermute(picked_small, AXES, downward)
    small_inner = lax.ppermute(small, AXES, inner)
    small_outer = lax.ppermute(small, AXES, outer)
    theta_inner = lax.ppermute(theta, AXES, inner)
    salt_inner = lax.ppermute(salt, AXES, inner)
    theta_outer = lax.ppermute(theta, AXES, outer)
    salt_outer = lax.ppermute(salt, AXES, outer)
    heights = lax.all_to_all(payload, AXES, 0, 0)
    pivots, part, token = pl.pallas_call(
        local_kernel,
        out_shape=(
            jax.ShapeDtypeStruct((3, 8 * levels, LANES), f32),
            jax.ShapeDtypeStruct((PART_WEIGHT + 8, cells), f32),
            jax.ShapeDtypeStruct((8, LANES), jnp.int32),
        ),
        in_specs=[HBM, HBM, VMEM, HBM, HBM],
        out_specs=(VMEM,) * 3,
        scratch_shapes=[
            vmem(levels, cells), vmem(levels, cells),
            vmem(levels - 1, cells), vmem(8, LANES, dtype=jnp.int32), vmem(8 * levels, LANES),
            vmem(5 * levels, cells, dtype=jnp.bfloat16), semaphores(4),
        ],
        compiler_params=grant(8),
        cost_estimate=estimate(2000000000, 4000000),
        name="local",
    )(*hbm(theta, salt), small, *hbm(kappa, depth8))
    small_below, small_above, small_inner, small_outer, heights, token, place = (
        lax.optimization_barrier(
            (small_below, small_above, small_inner, small_outer, heights, token, place)
        )
    )

    def subcycles(values, last):
        shape = jax.ShapeDtypeStruct((8, LANES), f32) if last else payload_shape
        return pl.pallas_call(
            functools.partial(surface_kernel, last=last),
            out_shape=shape,
            in_specs=[SMEM] + [VMEM] * 8,
            out_specs=VMEM,
            scratch_shapes=[vmem(8 * SMALL, LANES)] * 4
            + [vmem(32, LANES)] * 3
            + [vmem(32, 8, LANES)],
            compiler_params=grant(8),
            cost_estimate=estimate(2000000, 1000000),
            name="surface_last" if last else "surface_first",
        )(
            place, values, small, small_inner, small_outer, small_below, small_above, send4, token
        )

    heights2 = lax.all_to_all(subcycles(heights, False), AXES, 0, 0)
    surface = subcycles(heights2, True)
    theta_next, salt_next = pl.pallas_call(
        tracer_kernel,
        out_shape=(jax.ShapeDtypeStruct((levels, cells), f32),) * 2,
        in_specs=[SMEM] + [HBM] * 2 + [VMEM] * 13,
        out_specs=(HBM,) * 2,
        scratch_shapes=[
            vmem(2, levels, cells),
            vmem(5 * levels, 2 * cells + 2 * listed, dtype=jnp.bfloat16),
            vmem(2, 8 * levels, LANES), vmem(2, levels, cells), semaphores(2), semaphores(4),
        ],
        cost_estimate=estimate(4000000000, 8000000),
        compiler_params=grant(12),
        name="tracers",
    )(
        place, *hbm(theta, salt), small, theta_inner, salt_inner, small_inner, theta_outer,
        salt_outer, small_outer, below, small_below, above, small_above, pivots, part
    )
    return (theta_next, salt_next, surface.reshape(cells))


def solution(mesh):
    columns = P(None, AXES)
    cells = P(AXES)
    return jax.shard_map(
        functools.partial(body, mesh.shape["region"], mesh.shape["dom"]),
        mesh=mesh,
        in_specs=(columns, columns, cells, cells, columns, cells, columns, columns),
        out_specs=(columns, columns, cells),
        check_vma=False,
    )
```

```python
import functools
import math

import jax
import jax.numpy as jnp
from jax import lax
from jax.experimental import pallas as pl
from jax.experimental.pallas import tpu as pltpu
from jax.sharding import PartitionSpec as P

AXES = ("region", "dom")
LANES = 128
TILE = 256
ROW_DEPTH = 0
ROW_INDEX = 1
ROW_WEIGHT = 7
ROW_FORCING = 13
ROW_SURFACE = 14
SMALL = 16
PART_INDEX = 192
PART_WEIGHT = 200


def places(regions, doms):
    r = lax.axis_index("region")
    q = lax.axis_index("dom")

    def at(dr, dq):
        return lax.rem(r + dr + 2 * regions, regions) * doms + jnp.clip(q + dq, 0, doms - 1)

    return [
        at(0, 0), at(0, -2), at(0, -1), at(0, 1), at(0, 2),
        at(-1, -1), at(-1, 0), at(-1, 1), at(1, -1), at(1, 0), at(1, 1), at(-2, 0),
        q % 2 == 1, q >= 2, q >= 1, q < doms - 1, q < doms - 2, at(2, 0),
    ]


def lane_gather(source, lane):
    return jnp.take_along_axis(source, lane, axis=1, mode="promise_in_bounds")


def pick_block(source_rows, positions, blocks):
    lane = positions & (LANES - 1)
    block = positions >> 7
    result = lane_gather(source_rows(0), lane)
    for b in range(1, blocks):
        result = jnp.where(block == b, lane_gather(source_rows(b), lane), result)
    return result


def copies(pairs, semaphores):
    started = []
    for n, (source, target) in enumerate(pairs):
        copy = pltpu.make_async_copy(source, target, semaphores.at[n])
        copy.start()
        started.append(copy)
    return started


def pick_kernel(
    theta_in, salt_in, depth8, ssh8, neighbors, weights, send4,
    small, picked, picked_small, theta, salt, depths, heights, nbr, wts, sends, loaded
):
    levels, cells = theta.shape
    blocks = cells // LANES
    arrivals = copies(
        [
            (send4, sends), (ssh8, heights), (depth8, depths), (neighbors, nbr), (weights, wts),
            (theta_in, theta), (salt_in, salt),
        ],
        loaded,
    )
    for copy in arrivals[:5]:
        copy.wait()
    small[ROW_INDEX : ROW_INDEX + 6, :] = nbr[...].astype(jnp.float32)
    small[ROW_WEIGHT : ROW_WEIGHT + 6, :] = wts[...]
    small[SMALL - 1 : SMALL, :] = jnp.zeros((1, cells), jnp.float32)
    level = lax.broadcasted_iota(jnp.int32, (levels, LANES), 0)
    for b in range(blocks):
        cols = slice(b * LANES, (b + 1) * LANES)
        small[ROW_DEPTH : ROW_DEPTH + 1, cols] = depths[b : b + 1, :].astype(jnp.float32)
        small[ROW_SURFACE : ROW_SURFACE + 1, cols] = heights[b : b + 1, :]
    send_blocks = sends.shape[0]

    def pick(source, target, groups, offset):
        for t in range(send_blocks):
            positions = jnp.broadcast_to(sends[t : t + 1, :], (8, LANES))
            for r in range(groups):
                rows = slice(8 * r, 8 * r + 8)
                target[offset + 8 * r : offset + 8 * r + 8, t * LANES : (t + 1) * LANES] = pick_block(
                    lambda b: source[rows, b * LANES : (b + 1) * LANES], positions, blocks
                )

    arrivals[5].wait()
    pick(theta, picked, levels // 8, 0)
    arrivals[6].wait()
    pick(salt, picked, levels // 8, levels)
    for b in range(blocks):
        cols = slice(b * LANES, (b + 1) * LANES)
        term = 0.2 * theta[:, cols] - 0.15 * salt[:, cols]
        wet = level < depths[b : b + 1, :]
        total = jnp.sum(jnp.where(wet, term, 0.0), axis=0, keepdims=True)
        small[ROW_FORCING : ROW_FORCING + 1, cols] = total / math.sqrt(levels)
    pick(small, picked_small, SMALL // 8, 0)


def pack_kernel(theta, salt, ssh8, small, picked_small, message, payload, heights, loaded):
    levels = theta.shape[0]
    arrivals = copies(
        [
            (ssh8, heights),
            (theta, message.at[pl.ds(0, levels), :]),
            (salt, message.at[pl.ds(levels, levels), :]),
        ],
        loaded,
    )
    message[2 * levels :, :] = small[...]
    arrivals[0].wait()
    blocks = heights.shape[0]
    row = slice(ROW_SURFACE, ROW_SURFACE + 1)
    tail = jnp.concatenate(
        [
            picked_small[row, t * LANES : (t + 1) * LANES]
            for t in range(picked_small.shape[1] // LANES)
        ],
        axis=0,
    )
    send_all(payload, heights[...], tail)
    for copy in arrivals[1:]:
        copy.wait()


def send_all(payload, head, tail):
    blocks = head.shape[0]

    def send(i, carry):
        payload[i, 0:blocks, :] = head
        payload[i, blocks:, :] = tail
        return carry

    lax.fori_loop(0, payload.shape[0], send, 0)


def banded_step(ext, stat, own, sub):
    total = 0.25 * stat[8 * 13 : 8 * 14, :]
    for e in range(6):
        index = stat[8 * (1 + e) : 8 * (2 + e), :].astype(jnp.int32)
        weight = stat[8 * (7 + e) : 8 * (8 + e), :]
        lane = index & (LANES - 1)
        block = index >> 7
        key = jnp.where(block >= 24, block, block - sub)
        gathered = lane_gather(ext[0:8, :], lane)
        for d in range(1, 17):
            gathered = jnp.where(key == d, lane_gather(ext[d : d + 8, :], lane), gathered)
        for b in range(24, 32):
            row = jnp.broadcast_to(ext[b : b + 1, :], (8, LANES))
            gathered = jnp.where(key == b, lane_gather(row, lane), gathered)
        total = total + weight * (gathered - own)
    return own + total


def listed_step(ext, stat, own):
    total = 0.25 * stat[8 * 13 : 8 * 14, :]
    for e in range(6):
        index = stat[8 * (1 + e) : 8 * (2 + e), :].astype(jnp.int32)
        weight = stat[8 * (7 + e) : 8 * (8 + e), :]
        gathered = pick_block(lambda b: ext[b], index, 32)
        total = total + weight * (gathered - own)
    return own + total


def surface_kernel(
    below, above, heights, own_in, swap_in, swap_out, sends, pivots, part, out,
    stat_own, stat_left, stat_right, stat_list, ext_own, ext_left, ext_right, ext_list, *, last, shape
):
    blocks = own_in.shape[1] // LANES
    rest = slice(swap_in.shape[0] - SMALL, swap_in.shape[0])
    half = below.shape[1] // LANES
    place = places(*shape)
    odd = place[12]
    sub = lax.broadcasted_iota(jnp.int32, (8, LANES), 0)
    for b in range(blocks):
        cols = slice(b * LANES, (b + 1) * LANES)
        rows = pl.ds(b, SMALL, stride=8)
        first = swap_in[rest, cols]
        second = swap_out[rest, cols]
        stat_own[rows, :] = own_in[:, cols]
        stat_left[rows, :] = jnp.where(odd, first, second)
        stat_right[rows, :] = jnp.where(odd, second, first)
    for b in range(half):
        cols = slice(b * LANES, (b + 1) * LANES)
        stat_list[pl.ds(b, SMALL, stride=8), :] = below[:, cols]
        stat_list[pl.ds(half + b, SMALL, stride=8), :] = above[:, cols]

    def full(n, side):
        value = heights[place[n], 0:8, :]
        if side is None:
            return value
        return jnp.where(place[13 + side], value, 0.0)

    def listed(n):
        return heights[place[n], 8:12, :]

    own = full(0, None)
    left2, left, right, right2 = full(1, 0), full(2, 1), full(3, 2), full(4, 3)
    ext_own[0:8, :] = left
    ext_own[8:16, :] = own
    ext_own[16:24, :] = right
    ext_own[24:28, :] = listed(6)
    ext_own[28:32, :] = listed(9)
    ext_left[0:8, :] = left2
    ext_left[8:16, :] = left
    ext_left[16:24, :] = own
    ext_left[24:28, :] = listed(5)
    ext_left[28:32, :] = listed(8)
    ext_right[0:8, :] = own
    ext_right[8:16, :] = right
    ext_right[16:24, :] = right2
    ext_right[24:28, :] = listed(7)
    ext_right[28:32, :] = listed(10)
    low = sub < 4
    below_ext = [full(5, 1), full(6, None), full(7, 2)]
    above_ext = [full(8, 1), full(9, None), full(10, 2)]
    for part in range(3):
        for b in range(8):
            ext_list[8 * part + b] = jnp.where(
                low,
                jnp.broadcast_to(below_ext[part][b : b + 1, :], (8, LANES)),
                jnp.broadcast_to(above_ext[part][b : b + 1, :], (8, LANES)),
            )
    own_listed = listed(0)
    tails = [(listed(11), own_listed), (own_listed, listed(17))]
    for part in range(2):
        for b in range(4):
            ext_list[24 + 4 * part + b] = jnp.where(
                low,
                jnp.broadcast_to(tails[part][0][b : b + 1, :], (8, LANES)),
                jnp.broadcast_to(tails[part][1][b : b + 1, :], (8, LANES)),
            )
    own_list = jnp.concatenate([listed(6), listed(9)], axis=0)
    new_own = banded_step(ext_own, stat_own, own, sub)
    new_left = banded_step(ext_left, stat_left, left, sub)
    new_right = banded_step(ext_right, stat_right, right, sub)
    new_list = listed_step(ext_list, stat_list, own_list)
    ext_own[0:8, :] = jnp.where(place[14], new_left, 0.0)
    ext_own[8:16, :] = new_own
    ext_own[16:24, :] = jnp.where(place[15], new_right, 0.0)
    ext_own[24:32, :] = new_list
    final = banded_step(ext_own, stat_own, new_own, sub)
    if last:
        out[...] = final
        return
    ext_left[0:8, :] = final
    positions = jnp.concatenate([sends[...], sends[...]], axis=0)
    tail = pick_block(
        lambda b: jnp.broadcast_to(ext_left[b : b + 1, :], (8, LANES)), positions, blocks
    )

    send_all(out, final, tail[0:4, :])


def stage(sources, depth, target, width, offset, level):
    levels = level.shape[0]
    for b in range(width // LANES):
        cols = slice(b * LANES, (b + 1) * LANES)
        where = pl.ds(offset + b * LANES, LANES)
        wet = (level < depth[ROW_DEPTH : ROW_DEPTH + 1, cols]).astype(jnp.float32)
        for c in range(2):
            value = sources[c][:, cols] * wet
            high = value.astype(jnp.bfloat16)
            low = (value - high.astype(jnp.float32)).astype(jnp.bfloat16)
            target[c * levels : (c + 1) * levels, where] = low
            target[(2 + c) * levels : (3 + c) * levels, where] = high
        target[4 * levels : 5 * levels, where] = wet.astype(jnp.bfloat16)


def weight_tile(line, index, highs, lows, base):
    high = jnp.zeros((TILE, TILE), jnp.bfloat16)
    low = jnp.zeros((TILE, TILE), jnp.bfloat16)
    for e in range(6):
        local = index[e] - base
        local = jnp.where(jnp.logical_and(local >= 0, local < TILE), local, -1)
        local = local.astype(jnp.float32).astype(jnp.bfloat16)
        hit = line == local
        high = jnp.where(hit, highs[e], high)
        low = jnp.where(hit, lows[e], low)
    return high, low


def tile_line():
    line = lax.broadcasted_iota(jnp.int32, (TILE, TILE), 0)
    return line.astype(jnp.float32).astype(jnp.bfloat16)


def split_weights(rows, columns):
    weights = [rows[e : e + 1, columns] for e in range(6)]
    highs = [w.astype(jnp.bfloat16) for w in weights]
    lows = [(w - h.astype(jnp.float32)).astype(jnp.bfloat16) for w, h in zip(weights, highs)]
    return highs, lows


def product(rows, columns, high, low, levels):
    first = jnp.dot(rows[:, columns], high, preferred_element_type=jnp.float32)
    second = jnp.dot(rows[2 * levels :, columns], low, preferred_element_type=jnp.float32)
    return jnp.concatenate(
        [
            first[0 : 2 * levels] + first[2 * levels : 4 * levels] + second[0 : 2 * levels],
            first[4 * levels :] + second[2 * levels :],
        ],
        axis=0,
    )


def local_kernel(
    theta_in, salt_in, small, kappa_in, depth_in, pivots, part,
    theta, salt, kappa, depth8, kap, rows_own, loaded
):
    cells = small.shape[1]
    levels = pivots.shape[1] // 8
    arrivals = copies(
        [(depth_in, depth8), (kappa_in, kappa), (theta_in, theta), (salt_in, salt)], loaded
    )
    for copy in arrivals[:2]:
        copy.wait()
    for b in range(cells // LANES):
        cols = slice(b * LANES, (b + 1) * LANES)
        kap[pl.ds(b, levels - 1, stride=8), :] = kappa[:, cols]
    depth = depth8[...]
    before = jnp.zeros((8, LANES), jnp.float32)
    last_ratio = before
    for k in range(levels):
        rows = slice(8 * k, 8 * k + 8)
        if k < levels - 1:
            after = jnp.where(depth > k + 1, kap[rows, :], 0.0)
        else:
            after = jnp.zeros((8, LANES), jnp.float32)
        pivot = 1.0 + before + after - before * last_ratio
        inverse = 1.0 / pivot
        last_ratio = after * inverse
        pivots[0, rows, :] = last_ratio
        pivots[1, rows, :] = before * inverse
        pivots[2, rows, :] = inverse
        before = after
    index = [small[ROW_INDEX + e : ROW_INDEX + e + 1, :].astype(jnp.int32) for e in range(6)]
    weight = [small[ROW_WEIGHT + e : ROW_WEIGHT + e + 1, :] for e in range(6)]
    for e in range(5, 0, -1):
        taken = index[e] < 0
        for f in range(e):
            same = jnp.logical_and(index[e] == index[f], jnp.logical_not(taken))
            weight[f] = weight[f] + jnp.where(same, weight[e], 0.0)
            taken = jnp.logical_or(taken, same)
        index[e] = jnp.where(taken, -1, index[e])
    for e in range(6):
        part[PART_INDEX + e : PART_INDEX + e + 1, :] = index[e].astype(jnp.float32)
        part[PART_WEIGHT + e : PART_WEIGHT + e + 1, :] = weight[e]
    level = lax.broadcasted_iota(jnp.int32, (levels, LANES), 0).astype(jnp.float32)
    for copy in arrivals[2:]:
        copy.wait()
    stage((theta, salt), small, rows_own, cells, 0, level)
    line = tile_line()

    def block(t, carry):
        here = pl.ds(pl.multiple_of(t * TILE, TILE), TILE)
        idx = [part[PART_INDEX + e : PART_INDEX + e + 1, here].astype(jnp.int32) for e in range(6)]
        highs, lows = split_weights(part.at[pl.ds(PART_WEIGHT, 8), :], here)
        total = jnp.zeros((3 * levels, TILE), jnp.float32)
        for j in range(cells // TILE):
            high, low = weight_tile(line, idx, highs, lows, cells + j * TILE)
            columns = slice(j * TILE, (j + 1) * TILE)
            total = total + product(rows_own, columns, high, low, levels)
        part[0 : 3 * levels, here] = total
        return carry

    lax.fori_loop(0, cells // TILE, block, 0)


def tracer_kernel(
    theta_in, salt_in, small, small_below, small_above, below, above, swap_in, swap_out, pivots, part,
    theta_out, salt_out, own, rows_ext, star, result, loaded, stored
):
    levels, cells = theta_out.shape
    listed = below.shape[1]
    arrivals = copies([(theta_in, own.at[0]), (salt_in, own.at[1])], loaded)
    level = lax.broadcasted_iota(jnp.int32, (levels, LANES), 0).astype(jnp.float32)
    odd = lax.axis_index("dom") % 2 == 1
    inner = pl.multiple_of(jnp.where(odd, 0, cells), LANES)
    outer = pl.multiple_of(jnp.where(odd, cells, 0), LANES)
    starts = (inner, outer, 2 * cells, 2 * cells + listed)
    depths = [source.at[pl.ds(2 * levels, SMALL), :] for source in (swap_in, swap_out)]
    depths += [small_below, small_above]
    for source, depth, start in zip((swap_in, swap_out, below, above), depths, starts):
        tracers = [source.at[pl.ds(c * levels, levels), :] for c in range(2)]
        stage(tracers, depth, rows_ext, source.shape[1], start, level)
    for copy in arrivals:
        copy.wait()
    line = tile_line()
    band = (TILE + cells) // TILE
    region = 2 * listed // TILE

    def block(t, carry):
        start = pl.multiple_of(t * TILE, TILE)
        here = pl.ds(start, TILE)
        idx = []
        for e in range(6):
            value = part[PART_INDEX + e : PART_INDEX + e + 1, here].astype(jnp.int32)
            outside = jnp.where(value >= 2 * cells, value - cells, -1)
            idx.append(jnp.where(value < cells, value, outside))
        highs, lows = split_weights(part.at[pl.ds(PART_WEIGHT, 8), :], here)
        total = part[0 : 3 * levels, here]
        for j in range(band + region):
            base = start + j * TILE if j < band else 2 * cells + (j - band) * TILE
            base = pl.multiple_of(base, TILE)
            high, low = weight_tile(line, idx, highs, lows, base)
            total = total + product(rows_ext, pl.ds(base, TILE), high, low, levels)
        for b in range(TILE // LANES):
            cols = slice(b * LANES, (b + 1) * LANES)
            sub = pl.ds(start + b * LANES, LANES)
            wet = level < small[ROW_DEPTH : ROW_DEPTH + 1, sub]
            for c in range(2):
                value = own[c, :, sub]
                change = total[c * levels : (c + 1) * levels, cols] - value * total[2 * levels :, cols]
                stepped = value + jnp.where(wet, change, 0.0)
                star[c, pl.ds(t * (TILE // LANES) + b, levels, stride=8), :] = stepped
        return carry

    lax.fori_loop(0, cells // TILE, block, 0)
    for c in range(2):
        star[c] = star[c] * pivots[2]
    before = [star[0, 0:8, :], star[1, 0:8, :]]
    for k in range(1, levels):
        rows = slice(8 * k, 8 * k + 8)
        factor = pivots[1, rows, :]
        for c in range(2):
            before[c] = star[c, rows, :] + factor * before[c]
            star[c, rows, :] = before[c]
    for k in range(levels - 2, -1, -1):
        rows = slice(8 * k, 8 * k + 8)
        factor = pivots[0, rows, :]
        for c in range(2):
            before[c] = star[c, rows, :] + factor * before[c]
            star[c, rows, :] = before[c]
    departures = []
    for c, out in enumerate((theta_out, salt_out)):
        for b in range(cells // LANES):
            cols = slice(b * LANES, (b + 1) * LANES)
            result[c, :, cols] = star[c, pl.ds(b, levels, stride=8), :]
            if b % 4 == 3:
                done = pl.ds((b - 3) * LANES, 4 * LANES)
                departures += copies(
                    [(result.at[c, :, done], out.at[:, done])],
                    stored.at[pl.ds(2 * c + b // 4, 1)],
                )
    for copy in departures:
        copy.wait()


HBM = pl.BlockSpec(memory_space=pltpu.HBM)
VMEM = pl.BlockSpec(memory_space=pltpu.VMEM)


def grant(mebibytes):
    return pltpu.CompilerParams(vmem_limit_bytes=mebibytes * 1024 * 1024)


def estimate(flops, size):
    return pl.CostEstimate(flops=flops, bytes_accessed=size, transcendentals=0)


def body(regions, doms, theta, salt, ssh, depth, neighbors, send_list, weights, kappa):
    levels, cells = theta.shape
    listed = send_list.shape[0]
    devices = regions * doms
    f32 = jnp.float32
    depth8 = depth.reshape(cells // LANES, LANES)
    ssh8 = ssh.reshape(cells // LANES, LANES)
    send4 = send_list.reshape(listed // LANES, LANES)
    def vmem(*shape, dtype=f32):
        return pltpu.VMEM(shape, dtype)

    def semaphores(count):
        return pltpu.SemaphoreType.DMA((count,))

    payload_shape = jax.ShapeDtypeStruct((devices, 12, LANES), f32)

    def hbm(*arrays):
        return [pltpu.with_memory_space_constraint(array, pltpu.HBM) for array in arrays]

    small, picked, picked_small = pl.pallas_call(
        pick_kernel,
        out_shape=(
            jax.ShapeDtypeStruct((SMALL, cells), f32),
            jax.ShapeDtypeStruct((2 * levels, listed), f32),
            jax.ShapeDtypeStruct((SMALL, listed), f32),
        ),
        in_specs=[HBM] * 7,
        out_specs=(VMEM,) * 3,
        scratch_shapes=[
            vmem(levels, cells), vmem(levels, cells),
            vmem(8, LANES, dtype=jnp.int32), vmem(8, LANES), vmem(6, cells, dtype=jnp.int32),
            vmem(6, cells), vmem(listed // LANES, LANES, dtype=jnp.int32), semaphores(7),
        ],
        compiler_params=grant(8),
        cost_estimate=estimate(2000000, 2000000),
        name="pick",
    )(*hbm(theta, salt, depth8, ssh8, neighbors, weights, send4))
    message, payload = pl.pallas_call(
        pack_kernel,
        out_shape=(jax.ShapeDtypeStruct((2 * levels + SMALL, cells), f32), payload_shape),
        in_specs=[HBM] * 3 + [VMEM] * 2,
        out_specs=(VMEM,) * 2,
        scratch_shapes=[vmem(8, LANES), semaphores(3)],
        compiler_params=grant(8),
        cost_estimate=estimate(1000000, 2000000),
        name="pack",
    )(*hbm(theta, salt, ssh8), small, picked_small)

    def device(i, j):
        return (i % regions) * doms + j

    inner = [(device(i, j), device(i, j ^ 1)) for i in range(regions) for j in range(doms)]
    outer = [
        (device(i, j), device(i, j + 1 if j % 2 else j - 1))
        for i in range(regions)
        for j in range(1, doms - 1)
    ]
    upward = [(device(i, j), device(i + 1, j)) for i in range(regions) for j in range(doms)]
    downward = [(target, source) for source, target in upward]
    below = lax.ppermute(picked, AXES, upward)
    above = lax.ppermute(picked, AXES, downward)
    small_below = lax.ppermute(picked_small, AXES, upward)
    small_above = lax.ppermute(picked_small, AXES, downward)
    swap_in = lax.ppermute(message, AXES, inner)
    swap_out = lax.ppermute(message, AXES, outer)
    heights = lax.all_to_all(payload, AXES, 0, 0)
    pivots, part = pl.pallas_call(
        local_kernel,
        out_shape=(
            jax.ShapeDtypeStruct((3, 8 * levels, LANES), f32),
            jax.ShapeDtypeStruct((PART_WEIGHT + 8, cells), f32),
        ),
        in_specs=[HBM, HBM, VMEM, HBM, HBM],
        out_specs=(VMEM,) * 2,
        scratch_shapes=[
            vmem(levels, cells), vmem(levels, cells),
            vmem(levels - 1, cells), vmem(8, LANES, dtype=jnp.int32), vmem(8 * levels, LANES),
            vmem(5 * levels, cells, dtype=jnp.bfloat16), semaphores(4),
        ],
        compiler_params=grant(8),
        cost_estimate=estimate(40000000000, 4000000),
        name="local",
    )(*hbm(theta, salt), small, *hbm(kappa, depth8))
    small_below, small_above, swap_in, swap_out, heights, pivots, part = lax.optimization_barrier(
        (small_below, small_above, swap_in, swap_out, heights, pivots, part)
    )

    def subcycles(values, last):
        shape = jax.ShapeDtypeStruct((8, LANES), f32) if last else payload_shape
        return pl.pallas_call(
            functools.partial(surface_kernel, last=last, shape=(regions, doms)),
            out_shape=shape,
            in_specs=[VMEM] * 9,
            out_specs=VMEM,
            scratch_shapes=[vmem(8 * SMALL, LANES)] * 4
            + [vmem(32, LANES)] * 3
            + [vmem(32, 8, LANES)],
            compiler_params=grant(8),
            cost_estimate=estimate(1000, 1000),
            name="surface_last" if last else "surface_first",
        )(
            small_below, small_above, values, small, swap_in, swap_out, send4, pivots, part
        )

    heights2 = lax.all_to_all(subcycles(heights, False), AXES, 0, 0)
    surface = subcycles(heights2, True)
    theta_next, salt_next = pl.pallas_call(
        tracer_kernel,
        out_shape=(jax.ShapeDtypeStruct((levels, cells), f32),) * 2,
        in_specs=[HBM] * 2 + [VMEM] * 9,
        out_specs=(HBM,) * 2,
        scratch_shapes=[
            vmem(2, levels, cells),
            vmem(5 * levels, 2 * cells + 2 * listed, dtype=jnp.bfloat16),
            vmem(2, 8 * levels, LANES), vmem(2, levels, cells), semaphores(2), semaphores(4),
        ],
        cost_estimate=estimate(4000000000, 8000000),
        compiler_params=grant(12),
        name="tracers",
    )(
        *hbm(theta, salt), small, small_below, small_above, below, above, swap_in, swap_out,
        pivots, part
    )
    return (theta_next, salt_next, surface.reshape(cells))


def solution(mesh):
    columns = P(None, AXES)
    cells = P(AXES)
    return jax.shard_map(
        functools.partial(body, mesh.shape["region"], mesh.shape["dom"]),
        mesh=mesh,
        in_specs=(columns, columns, cells, cells, columns, cells, columns, columns),
        out_specs=(columns, columns, cells),
        check_vma=False,
    )
```

```python
import functools
import math

import jax
import jax.numpy as jnp
from jax import lax
from jax.experimental import pallas as pl
from jax.experimental.pallas import tpu as pltpu
from jax.sharding import PartitionSpec as P

AXES = ("region", "dom")
LANES = 128
TILE = 256
ROW_DEPTH = 0
ROW_INDEX = 1
ROW_WEIGHT = 7
ROW_FORCING = 13
ROW_SURFACE = 14
SMALL = 16
PART_INDEX = 0
PART_WEIGHT = 8


def places(regions, doms):
    r = lax.axis_index("region")
    q = lax.axis_index("dom")

    def at(dr, dq):
        return lax.rem(r + dr + 2 * regions, regions) * doms + jnp.clip(q + dq, 0, doms - 1)

    return [
        at(0, 0), at(0, -2), at(0, -1), at(0, 1), at(0, 2),
        at(-1, -1), at(-1, 0), at(-1, 1), at(1, -1), at(1, 0), at(1, 1), at(-2, 0),
        q % 2 == 1, q >= 2, q >= 1, q < doms - 1, q < doms - 2, at(2, 0),
    ]


def lane_gather(source, lane):
    return jnp.take_along_axis(source, lane, axis=1, mode="promise_in_bounds")


def pick_block(source_rows, positions, blocks):
    lane = positions & (LANES - 1)
    block = positions >> 7
    result = lane_gather(source_rows(0), lane)
    for b in range(1, blocks):
        result = jnp.where(block == b, lane_gather(source_rows(b), lane), result)
    return result


def copies(pairs, semaphores):
    started = []
    for n, (source, target) in enumerate(pairs):
        copy = pltpu.make_async_copy(source, target, semaphores.at[n])
        copy.start()
        started.append(copy)
    return started


def pick_kernel(
    theta_in, salt_in, depth8, ssh8, neighbors, weights, send4,
    small, picked, picked_small, message,
    theta, salt, depths, heights, nbr, wts, sends, loaded, stored
):
    levels, cells = theta.shape
    blocks = cells // LANES
    arrivals = copies(
        [
            (send4, sends), (ssh8, heights), (depth8, depths), (neighbors, nbr), (weights, wts),
            (theta_in, theta), (salt_in, salt),
        ],
        loaded,
    )
    for copy in arrivals[:5]:
        copy.wait()
    small[ROW_INDEX : ROW_INDEX + 6, :] = nbr[...].astype(jnp.float32)
    small[ROW_WEIGHT : ROW_WEIGHT + 6, :] = wts[...]
    small[SMALL - 1 : SMALL, :] = jnp.zeros((1, cells), jnp.float32)
    level = lax.broadcasted_iota(jnp.int32, (levels, LANES), 0)
    for b in range(blocks):
        cols = slice(b * LANES, (b + 1) * LANES)
        small[ROW_DEPTH : ROW_DEPTH + 1, cols] = depths[b : b + 1, :].astype(jnp.float32)
        small[ROW_SURFACE : ROW_SURFACE + 1, cols] = heights[b : b + 1, :]
    send_blocks = sends.shape[0]

    def pick(source, target, groups, offset):
        for t in range(send_blocks):
            positions = jnp.broadcast_to(sends[t : t + 1, :], (8, LANES))
            for r in range(groups):
                rows = slice(8 * r, 8 * r + 8)
                target[offset + 8 * r : offset + 8 * r + 8, t * LANES : (t + 1) * LANES] = pick_block(
                    lambda b: source[rows, b * LANES : (b + 1) * LANES], positions, blocks
                )

    departures = []
    for c, tracer in enumerate((theta, salt)):
        arrivals[5 + c].wait()
        target = message.at[pl.ds(c * levels, levels), :]
        departures += copies([(tracer, target)], stored.at[pl.ds(c, 1)])
    pick(theta, picked, levels // 8, 0)
    pick(salt, picked, levels // 8, levels)
    for b in range(blocks):
        cols = slice(b * LANES, (b + 1) * LANES)
        term = 0.2 * theta[:, cols] - 0.15 * salt[:, cols]
        wet = level < depths[b : b + 1, :]
        total = jnp.sum(jnp.where(wet, term, 0.0), axis=0, keepdims=True)
        small[ROW_FORCING : ROW_FORCING + 1, cols] = total / math.sqrt(levels)
    rest = message.at[pl.ds(2 * levels, SMALL), :]
    departures += copies([(small, rest)], stored.at[pl.ds(2, 1)])
    pick(small, picked_small, SMALL // 8, 0)
    for copy in departures:
        copy.wait()


def heights_kernel(ssh8, send4, payload_out, sends, heights, payload, loaded):
    for copy in copies([(ssh8, heights), (send4, sends)], loaded):
        copy.wait()
    broadcast_heights(heights[...], heights, sends, payload)
    for copy in copies([(payload, payload_out)], loaded.at[pl.ds(2, 1)]):
        copy.wait()


def broadcast_heights(own, rows, sends, payload):
    positions = jnp.concatenate([sends[...], sends[...]], axis=0)
    blocks = own.shape[0]
    tail = pick_block(
        lambda b: jnp.broadcast_to(rows[b : b + 1, :], (8, LANES)), positions, blocks
    )
    send_all(payload, own, tail[0 : sends.shape[0], :])


def send_all(payload, head, tail):
    def send(i, carry):
        payload[i, 0] = head[0:4, :]
        payload[i, 1] = head[4:8, :]
        payload[i, 2] = tail
        return carry

    lax.fori_loop(0, payload.shape[0], send, 0)


def banded_step(ext, stat, own, sub):
    total = 0.25 * stat[8 * 13 : 8 * 14, :]
    for e in range(6):
        index = stat[8 * (1 + e) : 8 * (2 + e), :].astype(jnp.int32)
        weight = stat[8 * (7 + e) : 8 * (8 + e), :]
        lane = index & (LANES - 1)
        block = index >> 7
        key = jnp.where(block >= 24, block, block - sub)
        gathered = lane_gather(ext[0:8, :], lane)
        for d in range(1, 17):
            gathered = jnp.where(key == d, lane_gather(ext[d : d + 8, :], lane), gathered)
        for b in range(24, 32):
            row = jnp.broadcast_to(ext[b : b + 1, :], (8, LANES))
            gathered = jnp.where(key == b, lane_gather(row, lane), gathered)
        total = total + weight * (gathered - own)
    return own + total


def listed_step(ext, stat, own):
    total = 0.25 * stat[8 * 13 : 8 * 14, :]
    for e in range(6):
        index = stat[8 * (1 + e) : 8 * (2 + e), :].astype(jnp.int32)
        weight = stat[8 * (7 + e) : 8 * (8 + e), :]
        gathered = pick_block(lambda b: ext[b], index, 32)
        total = total + weight * (gathered - own)
    return own + total


def surface_kernel(
    below, above, heights, own_in, swap_in, swap_out, sends, pivots, part, out_ref,
    stat_own, stat_left, stat_right, stat_list, ext_own, ext_left, ext_right, ext_list, out, stored,
    *, last, shape
):
    blocks = own_in.shape[1] // LANES
    rest = slice(swap_in.shape[0] - SMALL, swap_in.shape[0])
    half = below.shape[1] // LANES
    place = places(*shape)
    odd = place[12]
    sub = lax.broadcasted_iota(jnp.int32, (8, LANES), 0)
    for b in range(blocks):
        cols = slice(b * LANES, (b + 1) * LANES)
        rows = pl.ds(b, SMALL, stride=8)
        first = swap_in[rest, cols]
        second = swap_out[rest, cols]
        stat_own[rows, :] = own_in[:, cols]
        stat_left[rows, :] = jnp.where(odd, first, second)
        stat_right[rows, :] = jnp.where(odd, second, first)
    for b in range(half):
        cols = slice(b * LANES, (b + 1) * LANES)
        stat_list[pl.ds(b, SMALL, stride=8), :] = below[:, cols]
        stat_list[pl.ds(half + b, SMALL, stride=8), :] = above[:, cols]

    def full(n, side):
        value = jnp.concatenate([heights[place[n], 0], heights[place[n], 1]], axis=0)
        if side is None:
            return value
        return jnp.where(place[13 + side], value, 0.0)

    def listed(n):
        return heights[place[n], 2]

    own = full(0, None)
    left2, left, right, right2 = full(1, 0), full(2, 1), full(3, 2), full(4, 3)
    ext_own[0:8, :] = left
    ext_own[8:16, :] = own
    ext_own[16:24, :] = right
    ext_own[24:28, :] = listed(6)
    ext_own[28:32, :] = listed(9)
    ext_left[0:8, :] = left2
    ext_left[8:16, :] = left
    ext_left[16:24, :] = own
    ext_left[24:28, :] = listed(5)
    ext_left[28:32, :] = listed(8)
    ext_right[0:8, :] = own
    ext_right[8:16, :] = right
    ext_right[16:24, :] = right2
    ext_right[24:28, :] = listed(7)
    ext_right[28:32, :] = listed(10)
    low = sub < 4
    below_ext = [full(5, 1), full(6, None), full(7, 2)]
    above_ext = [full(8, 1), full(9, None), full(10, 2)]
    for part in range(3):
        for b in range(8):
            ext_list[8 * part + b] = jnp.where(
                low,
                jnp.broadcast_to(below_ext[part][b : b + 1, :], (8, LANES)),
                jnp.broadcast_to(above_ext[part][b : b + 1, :], (8, LANES)),
            )
    own_listed = listed(0)
    tails = [(listed(11), own_listed), (own_listed, listed(17))]
    for part in range(2):
        for b in range(4):
            ext_list[24 + 4 * part + b] = jnp.where(
                low,
                jnp.broadcast_to(tails[part][0][b : b + 1, :], (8, LANES)),
                jnp.broadcast_to(tails[part][1][b : b + 1, :], (8, LANES)),
            )
    own_list = jnp.concatenate([listed(6), listed(9)], axis=0)
    new_own = banded_step(ext_own, stat_own, own, sub)
    new_left = banded_step(ext_left, stat_left, left, sub)
    new_right = banded_step(ext_right, stat_right, right, sub)
    new_list = listed_step(ext_list, stat_list, own_list)
    ext_own[0:8, :] = jnp.where(place[14], new_left, 0.0)
    ext_own[8:16, :] = new_own
    ext_own[16:24, :] = jnp.where(place[15], new_right, 0.0)
    ext_own[24:32, :] = new_list
    final = banded_step(ext_own, stat_own, new_own, sub)
    if last:
        out_ref[...] = final
        return
    ext_left[0:8, :] = final
    broadcast_heights(final, ext_left, sends, out)
    for copy in copies([(out, out_ref)], stored):
        copy.wait()


def stage(sources, depth, target, width, offset, level):
    levels = level.shape[0]
    for b in range(width // LANES):
        cols = slice(b * LANES, (b + 1) * LANES)
        where = pl.ds(offset + b * LANES, LANES)
        wet = (level < depth[ROW_DEPTH : ROW_DEPTH + 1, cols]).astype(jnp.float32)
        for c in range(2):
            value = sources[c][:, cols] * wet
            high = value.astype(jnp.bfloat16)
            low = (value - high.astype(jnp.float32)).astype(jnp.bfloat16)
            target[c * levels : (c + 1) * levels, where] = low
            target[(2 + c) * levels : (3 + c) * levels, where] = high
        target[4 * levels : 5 * levels, where] = wet.astype(jnp.bfloat16)


def weight_tile(line, index, highs, lows, base, high, low, where):
    locals_ = []
    for e in range(6):
        local = index[e] - base
        local = jnp.where(jnp.logical_and(local >= 0, local < TILE), local, -1)
        locals_.append(local.astype(jnp.float32).astype(jnp.bfloat16))
    first = jnp.zeros((TILE, TILE), jnp.bfloat16)
    second = first
    for e in range(6):
        hit = line == locals_[e]
        first = jnp.where(hit, highs[e], first)
        second = jnp.where(hit, lows[e], second)
    high[where, :] = first
    low[where, :] = second


def tile_line():
    line = lax.broadcasted_iota(jnp.int32, (TILE, TILE), 0)
    return line.astype(jnp.float32).astype(jnp.bfloat16)


def split_weights(rows, columns):
    weights = [rows[e : e + 1, columns] for e in range(6)]
    highs = [w.astype(jnp.bfloat16) for w in weights]
    lows = [(w - h.astype(jnp.float32)).astype(jnp.bfloat16) for w, h in zip(weights, highs)]
    return highs, lows


def local_kernel(
    small, kappa_in, depth_in, pivots, part, kappa, depth8, kap, loaded
):
    cells = small.shape[1]
    levels = pivots.shape[1] // 8
    for copy in copies([(depth_in, depth8), (kappa_in, kappa)], loaded):
        copy.wait()
    for b in range(cells // LANES):
        cols = slice(b * LANES, (b + 1) * LANES)
        kap[pl.ds(b, levels - 1, stride=8), :] = kappa[:, cols]
    depth = depth8[...]
    before = jnp.zeros((8, LANES), jnp.float32)
    last_ratio = before
    for k in range(levels):
        rows = slice(8 * k, 8 * k + 8)
        if k < levels - 1:
            after = jnp.where(depth > k + 1, kap[rows, :], 0.0)
        else:
            after = jnp.zeros((8, LANES), jnp.float32)
        pivot = 1.0 + before + after - before * last_ratio
        inverse = 1.0 / pivot
        last_ratio = after * inverse
        pivots[0, rows, :] = last_ratio
        pivots[1, rows, :] = before * inverse
        pivots[2, rows, :] = inverse
        before = after
    index = [small[ROW_INDEX + e : ROW_INDEX + e + 1, :].astype(jnp.int32) for e in range(6)]
    weight = [small[ROW_WEIGHT + e : ROW_WEIGHT + e + 1, :] for e in range(6)]
    for e in range(5, 0, -1):
        taken = index[e] < 0
        for f in range(e):
            same = jnp.logical_and(index[e] == index[f], jnp.logical_not(taken))
            weight[f] = weight[f] + jnp.where(same, weight[e], 0.0)
            taken = jnp.logical_or(taken, same)
        index[e] = jnp.where(taken, -1, index[e])
    for e in range(6):
        part[PART_INDEX + e : PART_INDEX + e + 1, :] = index[e].astype(jnp.float32)
        part[PART_WEIGHT + e : PART_WEIGHT + e + 1, :] = weight[e]


def tracer_kernel(
    theta_in, salt_in, small, small_below, small_above, below, above, swap_in, swap_out, pivots,
    part, theta_out, salt_out, own, rows_ext, high, low, star, result, loaded, stored
):
    levels, cells = theta_out.shape
    listed = below.shape[1]
    arrivals = copies([(theta_in, own.at[0]), (salt_in, own.at[1])], loaded)
    level = lax.broadcasted_iota(jnp.int32, (levels, LANES), 0).astype(jnp.float32)
    odd = lax.axis_index("dom") % 2 == 1
    inner = pl.multiple_of(jnp.where(odd, 0, 2 * cells), LANES)
    outer = pl.multiple_of(jnp.where(odd, 2 * cells, 0), LANES)
    line = tile_line()
    band = (TILE + 2 * cells) // TILE
    region = 2 * listed // TILE

    def build(t, first, last):
        here = slice(t * TILE, (t + 1) * TILE)
        idx = [part[PART_INDEX + e : PART_INDEX + e + 1, here].astype(jnp.int32) for e in range(6)]
        highs, lows = split_weights(part.at[pl.ds(PART_WEIGHT, 8), :], here)
        for j in range(first, last):
            base = (t + j) * TILE if j < band else 3 * cells + (j - band) * TILE
            where = slice(j * TILE, (j + 1) * TILE)
            weight_tile(line, idx, highs, lows, base, high.at[t % 2], low.at[t % 2], where)

    middle = band // 2
    spans = ((0, middle), (middle, band), (band, band + region))

    def product(t):
        total = None
        for first, last in spans:
            if t + 1 < cells // TILE:
                build(t + 1, first, last)
            start = (t + first) * TILE if first < band else 3 * cells
            columns = slice(start, start + (last - first) * TILE)
            where = slice(first * TILE, last * TILE)
            upper = jnp.dot(
                rows_ext[:, columns], high[t % 2, where, :], preferred_element_type=jnp.float32
            )
            lower = jnp.dot(
                rows_ext[2 * levels :, columns], low[t % 2, where, :],
                preferred_element_type=jnp.float32,
            )
            values = upper[0 : 2 * levels] + upper[2 * levels : 4 * levels] + lower[0 : 2 * levels]
            wets = upper[4 * levels :] + lower[2 * levels :]
            total = (values, wets) if total is None else (total[0] + values, total[1] + wets)
        for b in range(TILE // LANES):
            cols = slice(b * LANES, (b + 1) * LANES)
            here = slice(t * TILE + b * LANES, t * TILE + (b + 1) * LANES)
            wet = level < small[ROW_DEPTH : ROW_DEPTH + 1, here]
            for c in range(2):
                value = own[c, :, here]
                change = total[0][c * levels : (c + 1) * levels, cols] - value * total[1][:, cols]
                stepped = value + jnp.where(wet, change, 0.0)
                star[c, pl.ds(t * (TILE // LANES) + b, levels, stride=8), :] = stepped

    build(0, 0, band + region)
    starts = (inner, outer, 3 * cells, 3 * cells + listed)
    depths = [source.at[pl.ds(2 * levels, SMALL), :] for source in (swap_in, swap_out)]
    depths += [small_below, small_above]
    for source, depth, start in zip((swap_in, swap_out, below, above), depths, starts):
        tracers = [source.at[pl.ds(c * levels, levels), :] for c in range(2)]
        stage(tracers, depth, rows_ext, source.shape[1], start, level)
    for copy in arrivals:
        copy.wait()
    stage((own.at[0], own.at[1]), small, rows_ext, cells, cells, level)
    for t in range(cells // TILE):
        product(t)
    for c in range(2):
        star[c] = star[c] * pivots[2]
    before = [star[0, 0:8, :], star[1, 0:8, :]]
    for k in range(1, levels):
        rows = slice(8 * k, 8 * k + 8)
        factor = pivots[1, rows, :]
        for c in range(2):
            before[c] = star[c, rows, :] + factor * before[c]
            star[c, rows, :] = before[c]
    for k in range(levels - 2, -1, -1):
        rows = slice(8 * k, 8 * k + 8)
        factor = pivots[0, rows, :]
        for c in range(2):
            before[c] = star[c, rows, :] + factor * before[c]
            star[c, rows, :] = before[c]
    departures = []
    for c, out in enumerate((theta_out, salt_out)):
        for b in range(cells // LANES):
            cols = slice(b * LANES, (b + 1) * LANES)
            result[c, :, cols] = star[c, pl.ds(b, levels, stride=8), :]
            if b % 4 == 3:
                done = pl.ds((b - 3) * LANES, 4 * LANES)
                departures += copies(
                    [(result.at[c, :, done], out.at[:, done])],
                    stored.at[pl.ds(2 * c + b // 4, 1)],
                )
    for copy in departures:
        copy.wait()


HBM = pl.BlockSpec(memory_space=pltpu.HBM)
VMEM = pl.BlockSpec(memory_space=pltpu.VMEM)


def grant(mebibytes):
    return pltpu.CompilerParams(vmem_limit_bytes=mebibytes * 1024 * 1024)


def estimate(flops, size):
    return pl.CostEstimate(flops=flops, bytes_accessed=size, transcendentals=0)


def body(regions, doms, theta, salt, ssh, depth, neighbors, send_list, weights, kappa):
    levels, cells = theta.shape
    listed = send_list.shape[0]
    devices = regions * doms
    f32 = jnp.float32
    depth8 = depth.reshape(cells // LANES, LANES)
    ssh8 = ssh.reshape(cells // LANES, LANES)
    send4 = send_list.reshape(listed // LANES, LANES)
    def vmem(*shape, dtype=f32):
        return pltpu.VMEM(shape, dtype)

    def semaphores(count):
        return pltpu.SemaphoreType.DMA((count,))

    payload_shape = jax.ShapeDtypeStruct((devices, 3, 4, LANES), f32)

    def hbm(*arrays):
        return [pltpu.with_memory_space_constraint(array, pltpu.HBM) for array in arrays]

    payload, sends = pl.pallas_call(
        heights_kernel,
        out_shape=(payload_shape, jax.ShapeDtypeStruct((listed // LANES, LANES), jnp.int32)),
        in_specs=[HBM] * 2,
        out_specs=(HBM, VMEM),
        scratch_shapes=[vmem(8, LANES), vmem(*payload_shape.shape), semaphores(3)],
        compiler_params=grant(8),
        cost_estimate=estimate(1000, 1000),
        name="heights",
    )(*hbm(ssh8, send4))
    small, picked, picked_small, message = pl.pallas_call(
        pick_kernel,
        out_shape=(
            jax.ShapeDtypeStruct((SMALL, cells), f32),
            jax.ShapeDtypeStruct((2 * levels, listed), f32),
            jax.ShapeDtypeStruct((SMALL, listed), f32),
            jax.ShapeDtypeStruct((2 * levels + SMALL, cells), f32),
        ),
        in_specs=[HBM] * 7,
        out_specs=(VMEM,) * 3 + (HBM,),
        scratch_shapes=[
            vmem(levels, cells), vmem(levels, cells),
            vmem(8, LANES, dtype=jnp.int32), vmem(8, LANES), vmem(6, cells, dtype=jnp.int32),
            vmem(6, cells), vmem(listed // LANES, LANES, dtype=jnp.int32), semaphores(7), semaphores(3),
        ],
        compiler_params=grant(8),
        cost_estimate=estimate(2000000, 2000000),
        name="pick",
    )(*hbm(theta, salt, depth8, ssh8, neighbors, weights, send4))
    def device(i, j):
        return (i % regions) * doms + j

    inner = [(device(i, j), device(i, j ^ 1)) for i in range(regions) for j in range(doms)]
    outer = [
        (device(i, j), device(i, j + 1 if j % 2 else j - 1))
        for i in range(regions)
        for j in range(1, doms - 1)
    ]
    upward = [(device(i, j), device(i + 1, j)) for i in range(regions) for j in range(doms)]
    downward = [(target, source) for source, target in upward]
    below = lax.ppermute(picked, AXES, upward)
    above = lax.ppermute(picked, AXES, downward)
    small_below = lax.ppermute(picked_small, AXES, upward)
    small_above = lax.ppermute(picked_small, AXES, downward)
    swap_in = lax.ppermute(message, AXES, inner)
    swap_out = lax.ppermute(message, AXES, outer)
    heights = lax.all_to_all(payload, AXES, 0, 0)
    heights, small_later = lax.optimization_barrier((heights, small))
    pivots, part = pl.pallas_call(
        local_kernel,
        out_shape=(
            jax.ShapeDtypeStruct((3, 8 * levels, LANES), f32),
            jax.ShapeDtypeStruct((PART_WEIGHT + 8, cells), f32),
        ),
        in_specs=[VMEM, HBM, HBM],
        out_specs=(VMEM,) * 2,
        scratch_shapes=[
            vmem(levels - 1, cells), vmem(8, LANES, dtype=jnp.int32), vmem(8 * levels, LANES),
            semaphores(2),
        ],
        compiler_params=grant(8),
        cost_estimate=estimate(40000000000, 4000000),
        name="local",
    )(small_later, *hbm(kappa, depth8))
    small_below, small_above, swap_in, swap_out, heights, pivots, part = lax.optimization_barrier(
        (small_below, small_above, swap_in, swap_out, heights, pivots, part)
    )

    def subcycles(values, last):
        shape = jax.ShapeDtypeStruct((8, LANES), f32) if last else payload_shape
        return pl.pallas_call(
            functools.partial(surface_kernel, last=last, shape=(regions, doms)),
            out_shape=shape,
            in_specs=[VMEM] * 9,
            out_specs=VMEM if last else HBM,
            scratch_shapes=[vmem(8 * SMALL, LANES)] * 4
            + [vmem(32, LANES)] * 3
            + [vmem(32, 8, LANES), vmem(*shape.shape), semaphores(1)],
            compiler_params=grant(8),
            cost_estimate=estimate(1000, 1000),
            name="surface_last" if last else "surface_first",
        )(
            small_below, small_above, values, small, swap_in, swap_out, sends, pivots, part
        )

    heights2 = lax.all_to_all(subcycles(heights, False), AXES, 0, 0)
    surface = subcycles(heights2, True)
    theta_next, salt_next = pl.pallas_call(
        tracer_kernel,
        out_shape=(jax.ShapeDtypeStruct((levels, cells), f32),) * 2,
        in_specs=[HBM] * 2 + [VMEM] * 9,
        out_specs=(HBM,) * 2,
        scratch_shapes=[
            vmem(2, levels, cells),
            vmem(5 * levels, 3 * cells + 2 * listed, dtype=jnp.bfloat16),
            vmem(2, TILE + 2 * cells + 2 * listed, TILE, dtype=jnp.bfloat16),
            vmem(2, TILE + 2 * cells + 2 * listed, TILE, dtype=jnp.bfloat16),
            vmem(2, 8 * levels, LANES), vmem(2, levels, cells), semaphores(2), semaphores(4),
        ],
        cost_estimate=estimate(4000000000, 8000000),
        compiler_params=grant(20),
        name="tracers",
    )(
        *hbm(theta, salt), small, small_below, small_above, below, above, swap_in, swap_out,
        pivots, part
    )
    return (theta_next, salt_next, surface.reshape(cells))


def solution(mesh):
    columns = P(None, AXES)
    cells = P(AXES)
    return jax.shard_map(
        functools.partial(body, mesh.shape["region"], mesh.shape["dom"]),
        mesh=mesh,
        in_specs=(columns, columns, cells, cells, columns, cells, columns, columns),
        out_specs=(columns, columns, cells),
        check_vma=False,
    )
```

```python
import functools
import math

import jax
import jax.numpy as jnp
from jax import lax
from jax.experimental import pallas as pl
from jax.experimental.pallas import tpu as pltpu
from jax.sharding import PartitionSpec as P

AXES = ("region", "dom")
LANES = 128
TILE = 256
ROW_DEPTH = 0
ROW_INDEX = 1
ROW_WEIGHT = 7
ROW_FORCING = 13
ROW_SURFACE = 14
SMALL = 16
PART_INDEX = 192
PART_WEIGHT = 200


def places(regions, doms):
    r = lax.axis_index("region")
    q = lax.axis_index("dom")

    def at(dr, dq):
        return lax.rem(r + dr + 2 * regions, regions) * doms + jnp.clip(q + dq, 0, doms - 1)

    return [
        at(0, 0), at(0, -2), at(0, -1), at(0, 1), at(0, 2),
        at(-1, -1), at(-1, 0), at(-1, 1), at(1, -1), at(1, 0), at(1, 1), at(-2, 0),
        q % 2 == 1, q >= 2, q >= 1, q < doms - 1, q < doms - 2, at(2, 0),
    ]


def lane_gather(source, lane):
    return jnp.take_along_axis(source, lane, axis=1, mode="promise_in_bounds")


def pick_block(source_rows, positions, blocks):
    lane = positions & (LANES - 1)
    block = positions >> 7
    result = lane_gather(source_rows(0), lane)
    for b in range(1, blocks):
        result = jnp.where(block == b, lane_gather(source_rows(b), lane), result)
    return result


def copies(pairs, semaphores):
    started = []
    for n, (source, target) in enumerate(pairs):
        copy = pltpu.make_async_copy(source, target, semaphores.at[n])
        copy.start()
        started.append(copy)
    return started


def pick_kernel(
    theta_in, salt_in, depth8, ssh8, neighbors, weights, send4,
    small, picked, picked_small, message,
    theta, salt, depths, heights, nbr, wts, sends, loaded, stored
):
    levels, cells = theta.shape
    blocks = cells // LANES
    arrivals = copies(
        [
            (send4, sends), (ssh8, heights), (depth8, depths), (neighbors, nbr), (weights, wts),
            (theta_in, theta), (salt_in, salt),
        ],
        loaded,
    )
    for copy in arrivals[:5]:
        copy.wait()
    small[ROW_INDEX : ROW_INDEX + 6, :] = nbr[...].astype(jnp.float32)
    small[ROW_WEIGHT : ROW_WEIGHT + 6, :] = wts[...]
    small[SMALL - 1 : SMALL, :] = jnp.zeros((1, cells), jnp.float32)
    level = lax.broadcasted_iota(jnp.int32, (levels, LANES), 0)
    for b in range(blocks):
        cols = slice(b * LANES, (b + 1) * LANES)
        small[ROW_DEPTH : ROW_DEPTH + 1, cols] = depths[b : b + 1, :].astype(jnp.float32)
        small[ROW_SURFACE : ROW_SURFACE + 1, cols] = heights[b : b + 1, :]
    send_blocks = sends.shape[0]

    def pick(source, target, groups, offset):
        for t in range(send_blocks):
            positions = jnp.broadcast_to(sends[t : t + 1, :], (8, LANES))
            for r in range(groups):
                rows = slice(8 * r, 8 * r + 8)
                target[offset + 8 * r : offset + 8 * r + 8, t * LANES : (t + 1) * LANES] = pick_block(
                    lambda b: source[rows, b * LANES : (b + 1) * LANES], positions, blocks
                )

    departures = []
    for c, tracer in enumerate((theta, salt)):
        arrivals[5 + c].wait()
        target = message.at[pl.ds(c * levels, levels), :]
        departures += copies([(tracer, target)], stored.at[pl.ds(c, 1)])
    pick(theta, picked, levels // 8, 0)
    pick(salt, picked, levels // 8, levels)
    for b in range(blocks):
        cols = slice(b * LANES, (b + 1) * LANES)
        term = 0.2 * theta[:, cols] - 0.15 * salt[:, cols]
        wet = level < depths[b : b + 1, :]
        total = jnp.sum(jnp.where(wet, term, 0.0), axis=0, keepdims=True)
        small[ROW_FORCING : ROW_FORCING + 1, cols] = total / math.sqrt(levels)
    rest = message.at[pl.ds(2 * levels, SMALL), :]
    departures += copies([(small, rest)], stored.at[pl.ds(2, 1)])
    pick(small, picked_small, SMALL // 8, 0)
    for copy in departures:
        copy.wait()


def heights_kernel(ssh8, send4, payload_out, sends, heights, payload, loaded):
    for copy in copies([(ssh8, heights), (send4, sends)], loaded):
        copy.wait()
    broadcast_heights(heights[...], heights, sends, payload)
    for copy in copies([(payload, payload_out)], loaded.at[pl.ds(2, 1)]):
        copy.wait()


def broadcast_heights(own, rows, sends, payload):
    positions = jnp.concatenate([sends[...], sends[...]], axis=0)
    blocks = own.shape[0]
    tail = pick_block(
        lambda b: jnp.broadcast_to(rows[b : b + 1, :], (8, LANES)), positions, blocks
    )
    send_all(payload, own, tail[0 : sends.shape[0], :])


def send_all(payload, head, tail):
    def send(i, carry):
        payload[i, 0] = head[0:4, :]
        payload[i, 1] = head[4:8, :]
        payload[i, 2] = tail
        return carry

    lax.fori_loop(0, payload.shape[0], send, 0)


def banded_step(ext, stat, own, sub):
    total = 0.25 * stat[8 * 13 : 8 * 14, :]
    for e in range(6):
        index = stat[8 * (1 + e) : 8 * (2 + e), :].astype(jnp.int32)
        weight = stat[8 * (7 + e) : 8 * (8 + e), :]
        lane = index & (LANES - 1)
        block = index >> 7
        key = jnp.where(block >= 24, block, block - sub)
        gathered = lane_gather(ext[0:8, :], lane)
        for d in range(1, 17):
            gathered = jnp.where(key == d, lane_gather(ext[d : d + 8, :], lane), gathered)
        for b in range(24, 32):
            row = jnp.broadcast_to(ext[b : b + 1, :], (8, LANES))
            gathered = jnp.where(key == b, lane_gather(row, lane), gathered)
        total = total + weight * (gathered - own)
    return own + total


def listed_step(ext, stat, own):
    total = 0.25 * stat[8 * 13 : 8 * 14, :]
    for e in range(6):
        index = stat[8 * (1 + e) : 8 * (2 + e), :].astype(jnp.int32)
        weight = stat[8 * (7 + e) : 8 * (8 + e), :]
        gathered = pick_block(lambda b: ext[b], index, 32)
        total = total + weight * (gathered - own)
    return own + total


def surface_kernel(
    below, above, heights, own_in, swap_in, swap_out, sends, pivots, part, out_ref,
    stat_own, stat_left, stat_right, stat_list, ext_own, ext_left, ext_right, ext_list, out, stored,
    *, last, shape
):
    blocks = own_in.shape[1] // LANES
    rest = slice(swap_in.shape[0] - SMALL, swap_in.shape[0])
    half = below.shape[1] // LANES
    place = places(*shape)
    odd = place[12]
    sub = lax.broadcasted_iota(jnp.int32, (8, LANES), 0)
    for b in range(blocks):
        cols = slice(b * LANES, (b + 1) * LANES)
        rows = pl.ds(b, SMALL, stride=8)
        first = swap_in[rest, cols]
        second = swap_out[rest, cols]
        stat_own[rows, :] = own_in[:, cols]
        stat_left[rows, :] = jnp.where(odd, first, second)
        stat_right[rows, :] = jnp.where(odd, second, first)
    for b in range(half):
        cols = slice(b * LANES, (b + 1) * LANES)
        stat_list[pl.ds(b, SMALL, stride=8), :] = below[:, cols]
        stat_list[pl.ds(half + b, SMALL, stride=8), :] = above[:, cols]

    def full(n, side):
        value = jnp.concatenate([heights[place[n], 0], heights[place[n], 1]], axis=0)
        if side is None:
            return value
        return jnp.where(place[13 + side], value, 0.0)

    def listed(n):
        return heights[place[n], 2]

    own = full(0, None)
    left2, left, right, right2 = full(1, 0), full(2, 1), full(3, 2), full(4, 3)
    ext_own[0:8, :] = left
    ext_own[8:16, :] = own
    ext_own[16:24, :] = right
    ext_own[24:28, :] = listed(6)
    ext_own[28:32, :] = listed(9)
    ext_left[0:8, :] = left2
    ext_left[8:16, :] = left
    ext_left[16:24, :] = own
    ext_left[24:28, :] = listed(5)
    ext_left[28:32, :] = listed(8)
    ext_right[0:8, :] = own
    ext_right[8:16, :] = right
    ext_right[16:24, :] = right2
    ext_right[24:28, :] = listed(7)
    ext_right[28:32, :] = listed(10)
    low = sub < 4
    below_ext = [full(5, 1), full(6, None), full(7, 2)]
    above_ext = [full(8, 1), full(9, None), full(10, 2)]
    for part in range(3):
        for b in range(8):
            ext_list[8 * part + b] = jnp.where(
                low,
                jnp.broadcast_to(below_ext[part][b : b + 1, :], (8, LANES)),
                jnp.broadcast_to(above_ext[part][b : b + 1, :], (8, LANES)),
            )
    own_listed = listed(0)
    tails = [(listed(11), own_listed), (own_listed, listed(17))]
    for part in range(2):
        for b in range(4):
            ext_list[24 + 4 * part + b] = jnp.where(
                low,
                jnp.broadcast_to(tails[part][0][b : b + 1, :], (8, LANES)),
                jnp.broadcast_to(tails[part][1][b : b + 1, :], (8, LANES)),
            )
    own_list = jnp.concatenate([listed(6), listed(9)], axis=0)
    new_own = banded_step(ext_own, stat_own, own, sub)
    new_left = banded_step(ext_left, stat_left, left, sub)
    new_right = banded_step(ext_right, stat_right, right, sub)
    new_list = listed_step(ext_list, stat_list, own_list)
    ext_own[0:8, :] = jnp.where(place[14], new_left, 0.0)
    ext_own[8:16, :] = new_own
    ext_own[16:24, :] = jnp.where(place[15], new_right, 0.0)
    ext_own[24:32, :] = new_list
    final = banded_step(ext_own, stat_own, new_own, sub)
    if last:
        out_ref[...] = final
        return
    ext_left[0:8, :] = final
    broadcast_heights(final, ext_left, sends, out)
    for copy in copies([(out, out_ref)], stored):
        copy.wait()


def stage(sources, depth, target, width, offset, level):
    levels = level.shape[0]
    for b in range(width // LANES):
        cols = slice(b * LANES, (b + 1) * LANES)
        where = pl.ds(offset + b * LANES, LANES)
        wet = (level < depth[ROW_DEPTH : ROW_DEPTH + 1, cols]).astype(jnp.float32)
        for c in range(2):
            value = sources[c][:, cols] * wet
            high = value.astype(jnp.bfloat16)
            low = (value - high.astype(jnp.float32)).astype(jnp.bfloat16)
            target[c * levels : (c + 1) * levels, where] = low
            target[(2 + c) * levels : (3 + c) * levels, where] = high
        target[4 * levels : 5 * levels, where] = wet.astype(jnp.bfloat16)


def weight_tile(line, index, highs, lows, base):
    high = jnp.zeros((TILE, TILE), jnp.bfloat16)
    low = jnp.zeros((TILE, TILE), jnp.bfloat16)
    for e in range(6):
        local = index[e] - base
        local = jnp.where(jnp.logical_and(local >= 0, local < TILE), local, -1)
        local = local.astype(jnp.float32).astype(jnp.bfloat16)
        hit = line == local
        high = jnp.where(hit, highs[e], high)
        low = jnp.where(hit, lows[e], low)
    return high, low


def tile_line():
    line = lax.broadcasted_iota(jnp.int32, (TILE, TILE), 0)
    return line.astype(jnp.float32).astype(jnp.bfloat16)


def split_weights(rows, columns):
    weights = [rows[e : e + 1, columns] for e in range(6)]
    highs = [w.astype(jnp.bfloat16) for w in weights]
    lows = [(w - h.astype(jnp.float32)).astype(jnp.bfloat16) for w, h in zip(weights, highs)]
    return highs, lows


def product(rows, columns, high, low, levels):
    first = jnp.dot(rows[:, columns], high, preferred_element_type=jnp.float32)
    second = jnp.dot(rows[2 * levels :, columns], low, preferred_element_type=jnp.float32)
    return jnp.concatenate(
        [
            first[0 : 2 * levels] + first[2 * levels : 4 * levels] + second[0 : 2 * levels],
            first[4 * levels :] + second[2 * levels :],
        ],
        axis=0,
    )


def local_kernel(
    theta_in, salt_in, small, kappa_in, depth_in, pivots, part,
    theta, salt, kappa, depth8, kap, rows_own, loaded
):
    cells = small.shape[1]
    levels = pivots.shape[1] // 8
    arrivals = copies(
        [(depth_in, depth8), (kappa_in, kappa), (theta_in, theta), (salt_in, salt)], loaded
    )
    for copy in arrivals[:2]:
        copy.wait()
    for b in range(cells // LANES):
        cols = slice(b * LANES, (b + 1) * LANES)
        kap[pl.ds(b, levels - 1, stride=8), :] = kappa[:, cols]
    depth = depth8[...]
    before = jnp.zeros((8, LANES), jnp.float32)
    last_ratio = before
    for k in range(levels):
        rows = slice(8 * k, 8 * k + 8)
        if k < levels - 1:
            after = jnp.where(depth > k + 1, kap[rows, :], 0.0)
        else:
            after = jnp.zeros((8, LANES), jnp.float32)
        pivot = 1.0 + before + after - before * last_ratio
        inverse = 1.0 / pivot
        last_ratio = after * inverse
        pivots[0, rows, :] = last_ratio
        pivots[1, rows, :] = before * inverse
        pivots[2, rows, :] = inverse
        before = after
    index = [small[ROW_INDEX + e : ROW_INDEX + e + 1, :].astype(jnp.int32) for e in range(6)]
    weight = [small[ROW_WEIGHT + e : ROW_WEIGHT + e + 1, :] for e in range(6)]
    for e in range(5, 0, -1):
        taken = index[e] < 0
        for f in range(e):
            same = jnp.logical_and(index[e] == index[f], jnp.logical_not(taken))
            weight[f] = weight[f] + jnp.where(same, weight[e], 0.0)
            taken = jnp.logical_or(taken, same)
        index[e] = jnp.where(taken, -1, index[e])
    for e in range(6):
        part[PART_INDEX + e : PART_INDEX + e + 1, :] = index[e].astype(jnp.float32)
        part[PART_WEIGHT + e : PART_WEIGHT + e + 1, :] = weight[e]
    level = lax.broadcasted_iota(jnp.int32, (levels, LANES), 0).astype(jnp.float32)
    for copy in arrivals[2:]:
        copy.wait()
    stage((theta, salt), small, rows_own, cells, 0, level)
    line = tile_line()

    def block(t, carry):
        here = pl.ds(pl.multiple_of(t * TILE, TILE), TILE)
        idx = [part[PART_INDEX + e : PART_INDEX + e + 1, here].astype(jnp.int32) for e in range(6)]
        highs, lows = split_weights(part.at[pl.ds(PART_WEIGHT, 8), :], here)
        total = jnp.zeros((3 * levels, TILE), jnp.float32)
        for j in range(cells // TILE):
            high, low = weight_tile(line, idx, highs, lows, cells + j * TILE)
            columns = slice(j * TILE, (j + 1) * TILE)
            total = total + product(rows_own, columns, high, low, levels)
        part[0 : 3 * levels, here] = total
        return carry

    lax.fori_loop(0, cells // TILE, block, 0)


def tracer_kernel(
    theta_in, salt_in, small, small_below, small_above, below, above, swap_in, swap_out, pivots, part,
    theta_out, salt_out, own, rows_ext, star, result, loaded, stored
):
    levels, cells = theta_out.shape
    listed = below.shape[1]
    arrivals = copies([(theta_in, own.at[0]), (salt_in, own.at[1])], loaded)
    level = lax.broadcasted_iota(jnp.int32, (levels, LANES), 0).astype(jnp.float32)
    odd = lax.axis_index("dom") % 2 == 1
    inner = pl.multiple_of(jnp.where(odd, 0, cells), LANES)
    outer = pl.multiple_of(jnp.where(odd, cells, 0), LANES)
    starts = (inner, outer, 2 * cells, 2 * cells + listed)
    depths = [source.at[pl.ds(2 * levels, SMALL), :] for source in (swap_in, swap_out)]
    depths += [small_below, small_above]
    for source, depth, start in zip((swap_in, swap_out, below, above), depths, starts):
        tracers = [source.at[pl.ds(c * levels, levels), :] for c in range(2)]
        stage(tracers, depth, rows_ext, source.shape[1], start, level)
    for copy in arrivals:
        copy.wait()
    line = tile_line()
    band = (TILE + cells) // TILE
    region = 2 * listed // TILE

    def block(t, carry):
        start = pl.multiple_of(t * TILE, TILE)
        here = pl.ds(start, TILE)
        idx = []
        for e in range(6):
            value = part[PART_INDEX + e : PART_INDEX + e + 1, here].astype(jnp.int32)
            outside = jnp.where(value >= 2 * cells, value - cells, -1)
            idx.append(jnp.where(value < cells, value, outside))
        highs, lows = split_weights(part.at[pl.ds(PART_WEIGHT, 8), :], here)
        total = part[0 : 3 * levels, here]
        for j in range(band + region):
            base = start + j * TILE if j < band else 2 * cells + (j - band) * TILE
            base = pl.multiple_of(base, TILE)
            high, low = weight_tile(line, idx, highs, lows, base)
            total = total + product(rows_ext, pl.ds(base, TILE), high, low, levels)
        for b in range(TILE // LANES):
            cols = slice(b * LANES, (b + 1) * LANES)
            sub = pl.ds(start + b * LANES, LANES)
            wet = level < small[ROW_DEPTH : ROW_DEPTH + 1, sub]
            for c in range(2):
                value = own[c, :, sub]
                change = total[c * levels : (c + 1) * levels, cols] - value * total[2 * levels :, cols]
                stepped = value + jnp.where(wet, change, 0.0)
                star[c, pl.ds(t * (TILE // LANES) + b, levels, stride=8), :] = stepped
        return carry

    lax.fori_loop(0, cells // TILE, block, 0)
    for c in range(2):
        star[c] = star[c] * pivots[2]
    before = [star[0, 0:8, :], star[1, 0:8, :]]
    for k in range(1, levels):
        rows = slice(8 * k, 8 * k + 8)
        factor = pivots[1, rows, :]
        for c in range(2):
            before[c] = star[c, rows, :] + factor * before[c]
            star[c, rows, :] = before[c]
    for k in range(levels - 2, -1, -1):
        rows = slice(8 * k, 8 * k + 8)
        factor = pivots[0, rows, :]
        for c in range(2):
            before[c] = star[c, rows, :] + factor * before[c]
            star[c, rows, :] = before[c]
    departures = []
    for c, out in enumerate((theta_out, salt_out)):
        for b in range(cells // LANES):
            cols = slice(b * LANES, (b + 1) * LANES)
            result[c, :, cols] = star[c, pl.ds(b, levels, stride=8), :]
            if b % 4 == 3:
                done = pl.ds((b - 3) * LANES, 4 * LANES)
                departures += copies(
                    [(result.at[c, :, done], out.at[:, done])],
                    stored.at[pl.ds(2 * c + b // 4, 1)],
                )
    for copy in departures:
        copy.wait()


HBM = pl.BlockSpec(memory_space=pltpu.HBM)
VMEM = pl.BlockSpec(memory_space=pltpu.VMEM)


def grant(mebibytes):
    return pltpu.CompilerParams(vmem_limit_bytes=mebibytes * 1024 * 1024)


def estimate(flops, size):
    return pl.CostEstimate(flops=flops, bytes_accessed=size, transcendentals=0)


def body(regions, doms, theta, salt, ssh, depth, neighbors, send_list, weights, kappa):
    levels, cells = theta.shape
    listed = send_list.shape[0]
    devices = regions * doms
    f32 = jnp.float32
    depth8 = depth.reshape(cells // LANES, LANES)
    ssh8 = ssh.reshape(cells // LANES, LANES)
    send4 = send_list.reshape(listed // LANES, LANES)
    def vmem(*shape, dtype=f32):
        return pltpu.VMEM(shape, dtype)

    def semaphores(count):
        return pltpu.SemaphoreType.DMA((count,))

    payload_shape = jax.ShapeDtypeStruct((devices, 3, 4, LANES), f32)

    def hbm(*arrays):
        return [pltpu.with_memory_space_constraint(array, pltpu.HBM) for array in arrays]

    payload, sends = pl.pallas_call(
        heights_kernel,
        out_shape=(payload_shape, jax.ShapeDtypeStruct((listed // LANES, LANES), jnp.int32)),
        in_specs=[HBM] * 2,
        out_specs=(HBM, VMEM),
        scratch_shapes=[vmem(8, LANES), vmem(*payload_shape.shape), semaphores(3)],
        compiler_params=grant(8),
        cost_estimate=estimate(1000, 1000),
        name="heights",
    )(*hbm(ssh8, send4))
    small, picked, picked_small, message = pl.pallas_call(
        pick_kernel,
        out_shape=(
            jax.ShapeDtypeStruct((SMALL, cells), f32),
            jax.ShapeDtypeStruct((2 * levels, listed), f32),
            jax.ShapeDtypeStruct((SMALL, listed), f32),
            jax.ShapeDtypeStruct((2 * levels + SMALL, cells), f32),
        ),
        in_specs=[HBM] * 7,
        out_specs=(VMEM,) * 3 + (HBM,),
        scratch_shapes=[
            vmem(levels, cells), vmem(levels, cells),
            vmem(8, LANES, dtype=jnp.int32), vmem(8, LANES), vmem(6, cells, dtype=jnp.int32),
            vmem(6, cells), vmem(listed // LANES, LANES, dtype=jnp.int32), semaphores(7), semaphores(3),
        ],
        compiler_params=grant(8),
        cost_estimate=estimate(2000000, 2000000),
        name="pick",
    )(*hbm(theta, salt, depth8, ssh8, neighbors, weights, send4))
    def device(i, j):
        return (i % regions) * doms + j

    inner = [(device(i, j), device(i, j ^ 1)) for i in range(regions) for j in range(doms)]
    outer = [
        (device(i, j), device(i, j + 1 if j % 2 else j - 1))
        for i in range(regions)
        for j in range(1, doms - 1)
    ]
    upward = [(device(i, j), device(i + 1, j)) for i in range(regions) for j in range(doms)]
    downward = [(target, source) for source, target in upward]
    below = lax.ppermute(picked, AXES, upward)
    above = lax.ppermute(picked, AXES, downward)
    small_below = lax.ppermute(picked_small, AXES, upward)
    small_above = lax.ppermute(picked_small, AXES, downward)
    swap_in = lax.ppermute(message, AXES, inner)
    swap_out = lax.ppermute(message, AXES, outer)
    heights = lax.all_to_all(payload, AXES, 0, 0)
    heights, small_later = lax.optimization_barrier((heights, small))
    pivots, part = pl.pallas_call(
        local_kernel,
        out_shape=(
            jax.ShapeDtypeStruct((3, 8 * levels, LANES), f32),
            jax.ShapeDtypeStruct((PART_WEIGHT + 8, cells), f32),
        ),
        in_specs=[HBM, HBM, VMEM, HBM, HBM],
        out_specs=(VMEM,) * 2,
        scratch_shapes=[
            vmem(levels, cells), vmem(levels, cells),
            vmem(levels - 1, cells), vmem(8, LANES, dtype=jnp.int32), vmem(8 * levels, LANES),
            vmem(5 * levels, cells, dtype=jnp.bfloat16), semaphores(4),
        ],
        compiler_params=grant(8),
        cost_estimate=estimate(40000000000, 4000000),
        name="local",
    )(*hbm(theta, salt), small_later, *hbm(kappa, depth8))
    small_below, small_above, swap_in, swap_out, heights, pivots, part = lax.optimization_barrier(
        (small_below, small_above, swap_in, swap_out, heights, pivots, part)
    )

    def subcycles(values, last):
        shape = jax.ShapeDtypeStruct((8, LANES), f32) if last else payload_shape
        return pl.pallas_call(
            functools.partial(surface_kernel, last=last, shape=(regions, doms)),
            out_shape=shape,
            in_specs=[VMEM] * 9,
            out_specs=VMEM if last else HBM,
            scratch_shapes=[vmem(8 * SMALL, LANES)] * 4
            + [vmem(32, LANES)] * 3
            + [vmem(32, 8, LANES), vmem(*shape.shape), semaphores(1)],
            compiler_params=grant(8),
            cost_estimate=estimate(1000, 1000),
            name="surface_last" if last else "surface_first",
        )(
            small_below, small_above, values, small, swap_in, swap_out, sends, pivots, part
        )

    heights2 = lax.all_to_all(subcycles(heights, False), AXES, 0, 0)
    surface = subcycles(heights2, True)
    theta_next, salt_next = pl.pallas_call(
        tracer_kernel,
        out_shape=(jax.ShapeDtypeStruct((levels, cells), f32),) * 2,
        in_specs=[HBM] * 2 + [VMEM] * 9,
        out_specs=(HBM,) * 2,
        scratch_shapes=[
            vmem(2, levels, cells),
            vmem(5 * levels, 2 * cells + 2 * listed, dtype=jnp.bfloat16),
            vmem(2, 8 * levels, LANES), vmem(2, levels, cells), semaphores(2), semaphores(4),
        ],
        cost_estimate=estimate(4000000000, 8000000),
        compiler_params=grant(12),
        name="tracers",
    )(
        *hbm(theta, salt), small, small_below, small_above, below, above, swap_in, swap_out,
        pivots, part
    )
    return (theta_next, salt_next, surface.reshape(cells))


def solution(mesh):
    columns = P(None, AXES)
    cells = P(AXES)
    return jax.shard_map(
        functools.partial(body, mesh.shape["region"], mesh.shape["dom"]),
        mesh=mesh,
        in_specs=(columns, columns, cells, cells, columns, cells, columns, columns),
        out_specs=(columns, columns, cells),
        check_vma=False,
    )
```

```python
import functools
import math

import jax
import jax.numpy as jnp
from jax import lax
from jax.experimental import pallas as pl
from jax.experimental.pallas import tpu as pltpu
from jax.sharding import PartitionSpec as P

AXES = ("region", "dom")
LANES = 128
TILE = 256
ROW_DEPTH = 0
ROW_INDEX = 1
ROW_WEIGHT = 7
ROW_FORCING = 13
ROW_SURFACE = 14
SMALL = 16
PARALLEL = 4
PART_INDEX = 192
PART_WEIGHT = 200


def places(regions, doms):
    r = lax.axis_index("region")
    q = lax.axis_index("dom")

    def at(dr, dq):
        return lax.rem(r + dr + 2 * regions, regions) * doms + jnp.clip(q + dq, 0, doms - 1)

    return [
        at(0, 0), at(0, -2), at(0, -1), at(0, 1), at(0, 2),
        at(-1, -1), at(-1, 0), at(-1, 1), at(1, -1), at(1, 0), at(1, 1), at(-2, 0),
        q % 2 == 1, q >= 2, q >= 1, q < doms - 1, q < doms - 2, at(2, 0),
    ]


def lane_gather(source, lane):
    return jnp.take_along_axis(source, lane, axis=1, mode="promise_in_bounds")


def pick_block(source_rows, positions, blocks):
    lane = positions & (LANES - 1)
    block = positions >> 7
    result = lane_gather(source_rows(0), lane)
    for b in range(1, blocks):
        result = jnp.where(block == b, lane_gather(source_rows(b), lane), result)
    return result


def copies(pairs, semaphores):
    started = []
    for n, (source, target) in enumerate(pairs):
        copy = pltpu.make_async_copy(source, target, semaphores.at[n])
        copy.start()
        started.append(copy)
    return started


def pick_kernel(
    theta_in, salt_in, depth8, ssh8, neighbors, weights, send4,
    small, picked, picked_small, message,
    theta, salt, depths, heights, nbr, wts, sends, loaded, stored
):
    levels, cells = theta.shape
    blocks = cells // LANES
    arrivals = copies(
        [
            (send4, sends), (ssh8, heights), (depth8, depths), (neighbors, nbr), (weights, wts),
            (theta_in, theta), (salt_in, salt),
        ],
        loaded,
    )
    for copy in arrivals[:5]:
        copy.wait()
    small[ROW_INDEX : ROW_INDEX + 6, :] = nbr[...].astype(jnp.float32)
    small[ROW_WEIGHT : ROW_WEIGHT + 6, :] = wts[...]
    small[SMALL - 1 : SMALL, :] = jnp.zeros((1, cells), jnp.float32)
    level = lax.broadcasted_iota(jnp.int32, (levels, LANES), 0)
    for b in range(blocks):
        cols = slice(b * LANES, (b + 1) * LANES)
        small[ROW_DEPTH : ROW_DEPTH + 1, cols] = depths[b : b + 1, :].astype(jnp.float32)
        small[ROW_SURFACE : ROW_SURFACE + 1, cols] = heights[b : b + 1, :]
    send_blocks = sends.shape[0]

    def pick(source, target, groups, offset):
        for t in range(send_blocks):
            positions = jnp.broadcast_to(sends[t : t + 1, :], (8, LANES))
            for r in range(groups):
                rows = slice(8 * r, 8 * r + 8)
                target[offset + 8 * r : offset + 8 * r + 8, t * LANES : (t + 1) * LANES] = pick_block(
                    lambda b: source[rows, b * LANES : (b + 1) * LANES], positions, blocks
                )

    departures = []
    for c, tracer in enumerate((theta, salt)):
        arrivals[5 + c].wait()
        target = message.at[pl.ds(c * levels, levels), :]
        departures += copies([(tracer, target)], stored.at[pl.ds(c, 1)])
    pick(theta, picked, levels // 8, 0)
    pick(salt, picked, levels // 8, levels)
    for b in range(blocks):
        cols = slice(b * LANES, (b + 1) * LANES)
        term = 0.2 * theta[:, cols] - 0.15 * salt[:, cols]
        wet = level < depths[b : b + 1, :]
        total = jnp.sum(jnp.where(wet, term, 0.0), axis=0, keepdims=True)
        small[ROW_FORCING : ROW_FORCING + 1, cols] = total / math.sqrt(levels)
    rest = message.at[pl.ds(2 * levels, SMALL), :]
    departures += copies([(small, rest)], stored.at[pl.ds(2, 1)])
    pick(small, picked_small, SMALL // 8, 0)
    for copy in departures:
        copy.wait()


def heights_kernel(ssh8, send4, payload_out, sends, heights, payload, loaded):
    for copy in copies([(ssh8, heights), (send4, sends)], loaded):
        copy.wait()
    broadcast_heights(heights[...], heights, sends, payload)
    send_payload(payload, payload_out, loaded.at[pl.ds(2, PARALLEL)])


def send_payload(source, target, semaphores):
    count = source.shape[0] // PARALLEL
    rows = [pl.ds(n * count, count) for n in range(PARALLEL)]
    for copy in copies([(source.at[part], target.at[part]) for part in rows], semaphores):
        copy.wait()


def broadcast_heights(own, rows, sends, payload):
    positions = jnp.concatenate([sends[...], sends[...]], axis=0)
    blocks = own.shape[0]
    tail = pick_block(
        lambda b: jnp.broadcast_to(rows[b : b + 1, :], (8, LANES)), positions, blocks
    )
    send_all(payload, own, tail[0 : sends.shape[0], :])


def send_all(payload, head, tail):
    def send(i, carry):
        payload[i, 0] = head[0:4, :]
        payload[i, 1] = head[4:8, :]
        payload[i, 2] = tail
        return carry

    lax.fori_loop(0, payload.shape[0], send, 0)


def banded_step(ext, stat, own, sub):
    total = 0.25 * stat[8 * 13 : 8 * 14, :]
    for e in range(6):
        index = stat[8 * (1 + e) : 8 * (2 + e), :].astype(jnp.int32)
        weight = stat[8 * (7 + e) : 8 * (8 + e), :]
        lane = index & (LANES - 1)
        block = index >> 7
        key = jnp.where(block >= 24, block, block - sub)
        gathered = lane_gather(ext[0:8, :], lane)
        for d in range(1, 17):
            gathered = jnp.where(key == d, lane_gather(ext[d : d + 8, :], lane), gathered)
        for b in range(24, 32):
            row = jnp.broadcast_to(ext[b : b + 1, :], (8, LANES))
            gathered = jnp.where(key == b, lane_gather(row, lane), gathered)
        total = total + weight * (gathered - own)
    return own + total


def listed_step(ext, stat, own):
    total = 0.25 * stat[8 * 13 : 8 * 14, :]
    for e in range(6):
        index = stat[8 * (1 + e) : 8 * (2 + e), :].astype(jnp.int32)
        weight = stat[8 * (7 + e) : 8 * (8 + e), :]
        gathered = pick_block(lambda b: ext[b], index, 32)
        total = total + weight * (gathered - own)
    return own + total


def surface_kernel(
    below, above, heights, own_in, swap_in, swap_out, sends, pivots, part, out_ref,
    stat_own, stat_left, stat_right, stat_list, ext_own, ext_left, ext_right, ext_list, out, stored,
    *, last, shape
):
    blocks = own_in.shape[1] // LANES
    rest = slice(swap_in.shape[0] - SMALL, swap_in.shape[0])
    half = below.shape[1] // LANES
    place = places(*shape)
    odd = place[12]
    sub = lax.broadcasted_iota(jnp.int32, (8, LANES), 0)
    for b in range(blocks):
        cols = slice(b * LANES, (b + 1) * LANES)
        rows = pl.ds(b, SMALL, stride=8)
        first = swap_in[rest, cols]
        second = swap_out[rest, cols]
        stat_own[rows, :] = own_in[:, cols]
        stat_left[rows, :] = jnp.where(odd, first, second)
        stat_right[rows, :] = jnp.where(odd, second, first)
    for b in range(half):
        cols = slice(b * LANES, (b + 1) * LANES)
        stat_list[pl.ds(b, SMALL, stride=8), :] = below[:, cols]
        stat_list[pl.ds(half + b, SMALL, stride=8), :] = above[:, cols]

    def full(n, side):
        value = jnp.concatenate([heights[place[n], 0], heights[place[n], 1]], axis=0)
        if side is None:
            return value
        return jnp.where(place[13 + side], value, 0.0)

    def listed(n):
        return heights[place[n], 2]

    own = full(0, None)
    left2, left, right, right2 = full(1, 0), full(2, 1), full(3, 2), full(4, 3)
    ext_own[0:8, :] = left
    ext_own[8:16, :] = own
    ext_own[16:24, :] = right
    ext_own[24:28, :] = listed(6)
    ext_own[28:32, :] = listed(9)
    ext_left[0:8, :] = left2
    ext_left[8:16, :] = left
    ext_left[16:24, :] = own
    ext_left[24:28, :] = listed(5)
    ext_left[28:32, :] = listed(8)
    ext_right[0:8, :] = own
    ext_right[8:16, :] = right
    ext_right[16:24, :] = right2
    ext_right[24:28, :] = listed(7)
    ext_right[28:32, :] = listed(10)
    low = sub < 4
    below_ext = [full(5, 1), full(6, None), full(7, 2)]
    above_ext = [full(8, 1), full(9, None), full(10, 2)]
    for part in range(3):
        for b in range(8):
            ext_list[8 * part + b] = jnp.where(
                low,
                jnp.broadcast_to(below_ext[part][b : b + 1, :], (8, LANES)),
                jnp.broadcast_to(above_ext[part][b : b + 1, :], (8, LANES)),
            )
    own_listed = listed(0)
    tails = [(listed(11), own_listed), (own_listed, listed(17))]
    for part in range(2):
        for b in range(4):
            ext_list[24 + 4 * part + b] = jnp.where(
                low,
                jnp.broadcast_to(tails[part][0][b : b + 1, :], (8, LANES)),
                jnp.broadcast_to(tails[part][1][b : b + 1, :], (8, LANES)),
            )
    own_list = jnp.concatenate([listed(6), listed(9)], axis=0)
    new_own = banded_step(ext_own, stat_own, own, sub)
    new_left = banded_step(ext_left, stat_left, left, sub)
    new_right = banded_step(ext_right, stat_right, right, sub)
    new_list = listed_step(ext_list, stat_list, own_list)
    ext_own[0:8, :] = jnp.where(place[14], new_left, 0.0)
    ext_own[8:16, :] = new_own
    ext_own[16:24, :] = jnp.where(place[15], new_right, 0.0)
    ext_own[24:32, :] = new_list
    final = banded_step(ext_own, stat_own, new_own, sub)
    if last:
        out_ref[...] = final
        return
    ext_left[0:8, :] = final
    broadcast_heights(final, ext_left, sends, out)
    send_payload(out, out_ref, stored)


def stage(sources, depth, target, width, offset, level):
    levels = level.shape[0]
    for b in range(width // LANES):
        cols = slice(b * LANES, (b + 1) * LANES)
        where = pl.ds(offset + b * LANES, LANES)
        wet = (level < depth[ROW_DEPTH : ROW_DEPTH + 1, cols]).astype(jnp.float32)
        for c in range(2):
            value = sources[c][:, cols] * wet
            high = value.astype(jnp.bfloat16)
            low = (value - high.astype(jnp.float32)).astype(jnp.bfloat16)
            target[c * levels : (c + 1) * levels, where] = low
            target[(2 + c) * levels : (3 + c) * levels, where] = high
        target[4 * levels : 5 * levels, where] = wet.astype(jnp.bfloat16)


def weight_tile(line, index, highs, lows, base):
    high = jnp.zeros((TILE, TILE), jnp.bfloat16)
    low = jnp.zeros((TILE, TILE), jnp.bfloat16)
    for e in range(6):
        local = index[e] - base
        local = jnp.where(jnp.logical_and(local >= 0, local < TILE), local, -1)
        local = local.astype(jnp.float32).astype(jnp.bfloat16)
        hit = line == local
        high = jnp.where(hit, highs[e], high)
        low = jnp.where(hit, lows[e], low)
    return high, low


def weight_tiles(line, index, highs, lows, base, count):
    tiles = [weight_tile(line, index, highs, lows, base + n * TILE) for n in range(count)]
    return tuple(jnp.concatenate([tile[part] for tile in tiles], axis=0) for part in range(2))


def tile_line():
    line = lax.broadcasted_iota(jnp.int32, (TILE, TILE), 0)
    return line.astype(jnp.float32).astype(jnp.bfloat16)


def split_weights(rows, columns):
    weights = [rows[e : e + 1, columns] for e in range(6)]
    highs = [w.astype(jnp.bfloat16) for w in weights]
    lows = [(w - h.astype(jnp.float32)).astype(jnp.bfloat16) for w, h in zip(weights, highs)]
    return highs, lows


def product(rows, columns, high, low, levels):
    first = jnp.dot(rows[:, columns], high, preferred_element_type=jnp.float32)
    second = jnp.dot(rows[2 * levels :, columns], low, preferred_element_type=jnp.float32)
    return jnp.concatenate(
        [
            first[0 : 2 * levels] + first[2 * levels : 4 * levels] + second[0 : 2 * levels],
            first[4 * levels :] + second[2 * levels :],
        ],
        axis=0,
    )


def local_kernel(
    theta_in, salt_in, small, kappa_in, depth_in, pivots, part,
    theta, salt, kappa, depth8, kap, rows_own, loaded
):
    cells = small.shape[1]
    levels = pivots.shape[1] // 8
    arrivals = copies(
        [(depth_in, depth8), (kappa_in, kappa), (theta_in, theta), (salt_in, salt)], loaded
    )
    for copy in arrivals[:2]:
        copy.wait()
    for b in range(cells // LANES):
        cols = slice(b * LANES, (b + 1) * LANES)
        kap[pl.ds(b, levels - 1, stride=8), :] = kappa[:, cols]
    depth = depth8[...]
    before = jnp.zeros((8, LANES), jnp.float32)
    last_ratio = before
    for k in range(levels):
        rows = slice(8 * k, 8 * k + 8)
        if k < levels - 1:
            after = jnp.where(depth > k + 1, kap[rows, :], 0.0)
        else:
            after = jnp.zeros((8, LANES), jnp.float32)
        pivot = 1.0 + before + after - before * last_ratio
        inverse = 1.0 / pivot
        last_ratio = after * inverse
        pivots[0, rows, :] = last_ratio
        pivots[1, rows, :] = before * inverse
        pivots[2, rows, :] = inverse
        before = after
    index = [small[ROW_INDEX + e : ROW_INDEX + e + 1, :].astype(jnp.int32) for e in range(6)]
    weight = [small[ROW_WEIGHT + e : ROW_WEIGHT + e + 1, :] for e in range(6)]
    for e in range(5, 0, -1):
        taken = index[e] < 0
        for f in range(e):
            same = jnp.logical_and(index[e] == index[f], jnp.logical_not(taken))
            weight[f] = weight[f] + jnp.where(same, weight[e], 0.0)
            taken = jnp.logical_or(taken, same)
        index[e] = jnp.where(taken, -1, index[e])
    for e in range(6):
        part[PART_INDEX + e : PART_INDEX + e + 1, :] = index[e].astype(jnp.float32)
        part[PART_WEIGHT + e : PART_WEIGHT + e + 1, :] = weight[e]
    level = lax.broadcasted_iota(jnp.int32, (levels, LANES), 0).astype(jnp.float32)
    for copy in arrivals[2:]:
        copy.wait()
    stage((theta, salt), small, rows_own, cells, 0, level)
    line = tile_line()

    def block(t, carry):
        here = pl.ds(pl.multiple_of(t * TILE, TILE), TILE)
        idx = [part[PART_INDEX + e : PART_INDEX + e + 1, here].astype(jnp.int32) for e in range(6)]
        highs, lows = split_weights(part.at[pl.ds(PART_WEIGHT, 8), :], here)
        total = jnp.zeros((3 * levels, TILE), jnp.float32)
        for j in range(0, cells // TILE, 2):
            high, low = weight_tiles(line, idx, highs, lows, cells + j * TILE, 2)
            columns = slice(j * TILE, (j + 2) * TILE)
            total = total + product(rows_own, columns, high, low, levels)
        part[0 : 3 * levels, here] = total
        return carry

    lax.fori_loop(0, cells // TILE, block, 0)


def tracer_kernel(
    theta_in, salt_in, small, small_below, small_above, below, above, swap_in, swap_out, pivots, part,
    theta_out, salt_out, own, rows_ext, star, result, loaded, stored
):
    levels, cells = theta_out.shape
    listed = below.shape[1]
    arrivals = copies([(theta_in, own.at[0]), (salt_in, own.at[1])], loaded)
    level = lax.broadcasted_iota(jnp.int32, (levels, LANES), 0).astype(jnp.float32)
    odd = lax.axis_index("dom") % 2 == 1
    inner = pl.multiple_of(jnp.where(odd, 0, cells), LANES)
    outer = pl.multiple_of(jnp.where(odd, cells, 0), LANES)
    starts = (inner, outer, 2 * cells, 2 * cells + listed)
    depths = [source.at[pl.ds(2 * levels, SMALL), :] for source in (swap_in, swap_out)]
    depths += [small_below, small_above]
    for source, depth, start in zip((swap_in, swap_out, below, above), depths, starts):
        tracers = [source.at[pl.ds(c * levels, levels), :] for c in range(2)]
        stage(tracers, depth, rows_ext, source.shape[1], start, level)
    for copy in arrivals:
        copy.wait()
    line = tile_line()
    band = (TILE + cells) // TILE
    region = 2 * listed // TILE

    def block(t, carry):
        start = pl.multiple_of(t * TILE, TILE)
        here = pl.ds(start, TILE)
        idx = []
        for e in range(6):
            value = part[PART_INDEX + e : PART_INDEX + e + 1, here].astype(jnp.int32)
            outside = jnp.where(value >= 2 * cells, value - cells, -1)
            idx.append(jnp.where(value < cells, value, outside))
        highs, lows = split_weights(part.at[pl.ds(PART_WEIGHT, 8), :], here)
        total = part[0 : 3 * levels, here]
        spans = [(start + j * TILE, min(3, band - j)) for j in range(0, band, 3)]
        spans += [(2 * cells + j * TILE, min(2, region - j)) for j in range(0, region, 2)]
        for base, count in spans:
            base = pl.multiple_of(base, TILE)
            high, low = weight_tiles(line, idx, highs, lows, base, count)
            total = total + product(rows_ext, pl.ds(base, count * TILE), high, low, levels)
        for b in range(TILE // LANES):
            cols = slice(b * LANES, (b + 1) * LANES)
            sub = pl.ds(start + b * LANES, LANES)
            wet = level < small[ROW_DEPTH : ROW_DEPTH + 1, sub]
            for c in range(2):
                value = own[c, :, sub]
                change = total[c * levels : (c + 1) * levels, cols] - value * total[2 * levels :, cols]
                stepped = value + jnp.where(wet, change, 0.0)
                star[c, pl.ds(t * (TILE // LANES) + b, levels, stride=8), :] = stepped
        return carry

    lax.fori_loop(0, cells // TILE, block, 0)
    for c in range(2):
        star[c] = star[c] * pivots[2]
    before = [star[0, 0:8, :], star[1, 0:8, :]]
    for k in range(1, levels):
        rows = slice(8 * k, 8 * k + 8)
        factor = pivots[1, rows, :]
        for c in range(2):
            before[c] = star[c, rows, :] + factor * before[c]
            star[c, rows, :] = before[c]
    for k in range(levels - 2, -1, -1):
        rows = slice(8 * k, 8 * k + 8)
        factor = pivots[0, rows, :]
        for c in range(2):
            before[c] = star[c, rows, :] + factor * before[c]
            star[c, rows, :] = before[c]
    departures = []
    for c, out in enumerate((theta_out, salt_out)):
        for b in range(cells // LANES):
            cols = slice(b * LANES, (b + 1) * LANES)
            result[c, :, cols] = star[c, pl.ds(b, levels, stride=8), :]
            if b % 4 == 3:
                done = pl.ds((b - 3) * LANES, 4 * LANES)
                departures += copies(
                    [(result.at[c, :, done], out.at[:, done])],
                    stored.at[pl.ds(2 * c + b // 4, 1)],
                )
    for copy in departures:
        copy.wait()


HBM = pl.BlockSpec(memory_space=pltpu.HBM)
VMEM = pl.BlockSpec(memory_space=pltpu.VMEM)


def grant(mebibytes):
    return pltpu.CompilerParams(vmem_limit_bytes=mebibytes * 1024 * 1024)


def estimate(flops, size):
    return pl.CostEstimate(flops=flops, bytes_accessed=size, transcendentals=0)


def body(regions, doms, theta, salt, ssh, depth, neighbors, send_list, weights, kappa):
    levels, cells = theta.shape
    listed = send_list.shape[0]
    devices = regions * doms
    f32 = jnp.float32
    depth8 = depth.reshape(cells // LANES, LANES)
    ssh8 = ssh.reshape(cells // LANES, LANES)
    send4 = send_list.reshape(listed // LANES, LANES)
    def vmem(*shape, dtype=f32):
        return pltpu.VMEM(shape, dtype)

    def semaphores(count):
        return pltpu.SemaphoreType.DMA((count,))

    payload_shape = jax.ShapeDtypeStruct((devices, 3, 4, LANES), f32)

    def hbm(*arrays):
        return [pltpu.with_memory_space_constraint(array, pltpu.HBM) for array in arrays]

    payload, sends = pl.pallas_call(
        heights_kernel,
        out_shape=(payload_shape, jax.ShapeDtypeStruct((listed // LANES, LANES), jnp.int32)),
        in_specs=[HBM] * 2,
        out_specs=(HBM, VMEM),
        scratch_shapes=[vmem(8, LANES), vmem(*payload_shape.shape), semaphores(2 + PARALLEL)],
        compiler_params=grant(8),
        cost_estimate=estimate(1000, 1000),
        name="heights",
    )(*hbm(ssh8, send4))
    small, picked, picked_small, message = pl.pallas_call(
        pick_kernel,
        out_shape=(
            jax.ShapeDtypeStruct((SMALL, cells), f32),
            jax.ShapeDtypeStruct((2 * levels, listed), f32),
            jax.ShapeDtypeStruct((SMALL, listed), f32),
            jax.ShapeDtypeStruct((2 * levels + SMALL, cells), f32),
        ),
        in_specs=[HBM] * 7,
        out_specs=(VMEM,) * 3 + (HBM,),
        scratch_shapes=[
            vmem(levels, cells), vmem(levels, cells),
            vmem(8, LANES, dtype=jnp.int32), vmem(8, LANES), vmem(6, cells, dtype=jnp.int32),
            vmem(6, cells), vmem(listed // LANES, LANES, dtype=jnp.int32), semaphores(7), semaphores(3),
        ],
        compiler_params=grant(8),
        cost_estimate=estimate(2000000, 2000000),
        name="pick",
    )(*hbm(theta, salt, depth8, ssh8, neighbors, weights, send4))
    def device(i, j):
        return (i % regions) * doms + j

    inner = [(device(i, j), device(i, j ^ 1)) for i in range(regions) for j in range(doms)]
    outer = [
        (device(i, j), device(i, j + 1 if j % 2 else j - 1))
        for i in range(regions)
        for j in range(1, doms - 1)
    ]
    upward = [(device(i, j), device(i + 1, j)) for i in range(regions) for j in range(doms)]
    downward = [(target, source) for source, target in upward]
    below = lax.ppermute(picked, AXES, upward)
    above = lax.ppermute(picked, AXES, downward)
    small_below = lax.ppermute(picked_small, AXES, upward)
    small_above = lax.ppermute(picked_small, AXES, downward)
    swap_in = lax.ppermute(message, AXES, inner)
    swap_out = lax.ppermute(message, AXES, outer)
    heights = lax.all_to_all(payload, AXES, 0, 0)
    heights, small_later = lax.optimization_barrier((heights, small))
    pivots, part = pl.pallas_call(
        local_kernel,
        out_shape=(
            jax.ShapeDtypeStruct((3, 8 * levels, LANES), f32),
            jax.ShapeDtypeStruct((PART_WEIGHT + 8, cells), f32),
        ),
        in_specs=[HBM, HBM, VMEM, HBM, HBM],
        out_specs=(VMEM,) * 2,
        scratch_shapes=[
            vmem(levels, cells), vmem(levels, cells),
            vmem(levels - 1, cells), vmem(8, LANES, dtype=jnp.int32), vmem(8 * levels, LANES),
            vmem(5 * levels, cells, dtype=jnp.bfloat16), semaphores(4),
        ],
        compiler_params=grant(8),
        cost_estimate=estimate(40000000000, 4000000),
        name="local",
    )(*hbm(theta, salt), small_later, *hbm(kappa, depth8))
    small_below, small_above, swap_in, swap_out, heights, pivots, part = lax.optimization_barrier(
        (small_below, small_above, swap_in, swap_out, heights, pivots, part)
    )

    def subcycles(values, last):
        shape = jax.ShapeDtypeStruct((8, LANES), f32) if last else payload_shape
        return pl.pallas_call(
            functools.partial(surface_kernel, last=last, shape=(regions, doms)),
            out_shape=shape,
            in_specs=[VMEM] * 9,
            out_specs=VMEM if last else HBM,
            scratch_shapes=[vmem(8 * SMALL, LANES)] * 4
            + [vmem(32, LANES)] * 3
            + [vmem(32, 8, LANES), vmem(*shape.shape), semaphores(PARALLEL)],
            compiler_params=grant(8),
            cost_estimate=estimate(1000, 1000),
            name="surface_last" if last else "surface_first",
        )(
            small_below, small_above, values, small, swap_in, swap_out, sends, pivots, part
        )

    heights2 = lax.all_to_all(subcycles(heights, False), AXES, 0, 0)
    surface = subcycles(heights2, True)
    theta_next, salt_next = pl.pallas_call(
        tracer_kernel,
        out_shape=(jax.ShapeDtypeStruct((levels, cells), f32),) * 2,
        in_specs=[HBM] * 2 + [VMEM] * 9,
        out_specs=(HBM,) * 2,
        scratch_shapes=[
            vmem(2, levels, cells),
            vmem(5 * levels, 2 * cells + 2 * listed, dtype=jnp.bfloat16),
            vmem(2, 8 * levels, LANES), vmem(2, levels, cells), semaphores(2), semaphores(4),
        ],
        cost_estimate=estimate(4000000000, 8000000),
        compiler_params=grant(12),
        name="tracers",
    )(
        *hbm(theta, salt), small, small_below, small_above, below, above, swap_in, swap_out,
        pivots, part
    )
    return (theta_next, salt_next, surface.reshape(cells))


def solution(mesh):
    columns = P(None, AXES)
    cells = P(AXES)
    return jax.shard_map(
        functools.partial(body, mesh.shape["region"], mesh.shape["dom"]),
        mesh=mesh,
        in_specs=(columns, columns, cells, cells, columns, cells, columns, columns),
        out_specs=(columns, columns, cells),
        check_vma=False,
    )
```

```python
import functools
import math

import jax
import jax.numpy as jnp
from jax import lax
from jax.experimental import pallas as pl
from jax.experimental.pallas import tpu as pltpu
from jax.sharding import PartitionSpec as P

AXES = ("region", "dom")
LANES = 128
TILE = 256
ROW_DEPTH = 0
ROW_INDEX = 1
ROW_WEIGHT = 7
ROW_FORCING = 13
ROW_SURFACE = 14
SMALL = 16
PARALLEL = 4
PART_INDEX = 192
PART_WEIGHT = 200


def places(regions, doms):
    r = lax.axis_index("region")
    q = lax.axis_index("dom")

    def at(dr, dq):
        return lax.rem(r + dr + 2 * regions, regions) * doms + jnp.clip(q + dq, 0, doms - 1)

    return [
        at(0, 0), at(0, -2), at(0, -1), at(0, 1), at(0, 2),
        at(-1, -1), at(-1, 0), at(-1, 1), at(1, -1), at(1, 0), at(1, 1), at(-2, 0),
        q % 2 == 1, q >= 2, q >= 1, q < doms - 1, q < doms - 2, at(2, 0),
    ]


def lane_gather(source, lane):
    return jnp.take_along_axis(source, lane, axis=1, mode="promise_in_bounds")


def pick_block(source_rows, positions, blocks):
    lane = positions & (LANES - 1)
    block = positions >> 7
    result = lane_gather(source_rows(0), lane)
    for b in range(1, blocks):
        result = jnp.where(block == b, lane_gather(source_rows(b), lane), result)
    return result


def copies(pairs, semaphores):
    started = []
    for n, (source, target) in enumerate(pairs):
        copy = pltpu.make_async_copy(source, target, semaphores.at[n])
        copy.start()
        started.append(copy)
    return started


def pick_kernel(
    theta_in, salt_in, depth8, ssh8, neighbors, weights, send4,
    small, picked, picked_small, message,
    theta, salt, depths, heights, nbr, wts, sends, loaded, stored
):
    levels, cells = theta.shape
    blocks = cells // LANES
    arrivals = copies(
        [
            (send4, sends), (ssh8, heights), (depth8, depths), (neighbors, nbr), (weights, wts),
            (theta_in, theta), (salt_in, salt),
        ],
        loaded,
    )
    for copy in arrivals[:5]:
        copy.wait()
    small[ROW_INDEX : ROW_INDEX + 6, :] = nbr[...].astype(jnp.float32)
    small[ROW_WEIGHT : ROW_WEIGHT + 6, :] = wts[...]
    small[SMALL - 1 : SMALL, :] = jnp.zeros((1, cells), jnp.float32)
    level = lax.broadcasted_iota(jnp.int32, (levels, LANES), 0)
    for b in range(blocks):
        cols = slice(b * LANES, (b + 1) * LANES)
        small[ROW_DEPTH : ROW_DEPTH + 1, cols] = depths[b : b + 1, :].astype(jnp.float32)
        small[ROW_SURFACE : ROW_SURFACE + 1, cols] = heights[b : b + 1, :]
    send_blocks = sends.shape[0]

    def pick(source, target, groups, offset):
        for t in range(send_blocks):
            positions = jnp.broadcast_to(sends[t : t + 1, :], (8, LANES))
            for r in range(groups):
                rows = slice(8 * r, 8 * r + 8)
                target[offset + 8 * r : offset + 8 * r + 8, t * LANES : (t + 1) * LANES] = pick_block(
                    lambda b: source[rows, b * LANES : (b + 1) * LANES], positions, blocks
                )

    departures = []
    for c, tracer in enumerate((theta, salt)):
        arrivals[5 + c].wait()
        target = message.at[pl.ds(c * levels, levels), :]
        departures += copies([(tracer, target)], stored.at[pl.ds(c, 1)])
        if c == 0:
            pick(theta, picked, levels // 8, 0)
    for b in range(blocks):
        cols = slice(b * LANES, (b + 1) * LANES)
        term = 0.2 * theta[:, cols] - 0.15 * salt[:, cols]
        wet = level < depths[b : b + 1, :]
        total = jnp.sum(jnp.where(wet, term, 0.0), axis=0, keepdims=True)
        small[ROW_FORCING : ROW_FORCING + 1, cols] = total / math.sqrt(levels)
    rest = message.at[pl.ds(2 * levels, SMALL), :]
    departures += copies([(small, rest)], stored.at[pl.ds(2, 1)])
    pick(salt, picked, levels // 8, levels)
    pick(small, picked_small, SMALL // 8, 0)
    for copy in departures:
        copy.wait()


def heights_kernel(ssh8, send4, payload_out, sends, heights, payload, loaded):
    for copy in copies([(ssh8, heights), (send4, sends)], loaded):
        copy.wait()
    broadcast_heights(heights[...], heights, sends, payload)
    send_payload(payload, payload_out, loaded.at[pl.ds(2, PARALLEL)])


def send_payload(source, target, semaphores):
    count = source.shape[0] // PARALLEL
    rows = [pl.ds(n * count, count) for n in range(PARALLEL)]
    for copy in copies([(source.at[part], target.at[part]) for part in rows], semaphores):
        copy.wait()


def broadcast_heights(own, rows, sends, payload):
    positions = jnp.concatenate([sends[...], sends[...]], axis=0)
    blocks = own.shape[0]
    tail = pick_block(
        lambda b: jnp.broadcast_to(rows[b : b + 1, :], (8, LANES)), positions, blocks
    )
    send_all(payload, own, tail[0 : sends.shape[0], :])


def send_all(payload, head, tail):
    def send(i, carry):
        payload[i, 0] = head[0:4, :]
        payload[i, 1] = head[4:8, :]
        payload[i, 2] = tail
        return carry

    lax.fori_loop(0, payload.shape[0], send, 0)


def banded_step(ext, stat, own, sub):
    total = 0.25 * stat[8 * 13 : 8 * 14, :]
    for e in range(6):
        index = stat[8 * (1 + e) : 8 * (2 + e), :].astype(jnp.int32)
        weight = stat[8 * (7 + e) : 8 * (8 + e), :]
        lane = index & (LANES - 1)
        block = index >> 7
        key = jnp.where(block >= 24, block, block - sub)
        gathered = lane_gather(ext[0:8, :], lane)
        for d in range(1, 17):
            gathered = jnp.where(key == d, lane_gather(ext[d : d + 8, :], lane), gathered)
        for b in range(24, 32):
            row = jnp.broadcast_to(ext[b : b + 1, :], (8, LANES))
            gathered = jnp.where(key == b, lane_gather(row, lane), gathered)
        total = total + weight * (gathered - own)
    return own + total


def listed_step(ext, stat, own):
    total = 0.25 * stat[8 * 13 : 8 * 14, :]
    for e in range(6):
        index = stat[8 * (1 + e) : 8 * (2 + e), :].astype(jnp.int32)
        weight = stat[8 * (7 + e) : 8 * (8 + e), :]
        gathered = pick_block(lambda b: ext[b], index, 32)
        total = total + weight * (gathered - own)
    return own + total


def surface_kernel(
    below, above, heights, own_in, swap_in, swap_out, sends, pivots, part, out_ref,
    stat_own, stat_left, stat_right, stat_list, ext_own, ext_left, ext_right, ext_list, out, stored,
    *, last, shape
):
    blocks = own_in.shape[1] // LANES
    rest = slice(swap_in.shape[0] - SMALL, swap_in.shape[0])
    half = below.shape[1] // LANES
    place = places(*shape)
    odd = place[12]
    sub = lax.broadcasted_iota(jnp.int32, (8, LANES), 0)
    for b in range(blocks):
        cols = slice(b * LANES, (b + 1) * LANES)
        rows = pl.ds(b, SMALL, stride=8)
        first = swap_in[rest, cols]
        second = swap_out[rest, cols]
        stat_own[rows, :] = own_in[:, cols]
        stat_left[rows, :] = jnp.where(odd, first, second)
        stat_right[rows, :] = jnp.where(odd, second, first)
    for b in range(half):
        cols = slice(b * LANES, (b + 1) * LANES)
        stat_list[pl.ds(b, SMALL, stride=8), :] = below[:, cols]
        stat_list[pl.ds(half + b, SMALL, stride=8), :] = above[:, cols]

    def full(n, side):
        value = jnp.concatenate([heights[place[n], 0], heights[place[n], 1]], axis=0)
        if side is None:
            return value
        return jnp.where(place[13 + side], value, 0.0)

    def listed(n):
        return heights[place[n], 2]

    own = full(0, None)
    left2, left, right, right2 = full(1, 0), full(2, 1), full(3, 2), full(4, 3)
    ext_own[0:8, :] = left
    ext_own[8:16, :] = own
    ext_own[16:24, :] = right
    ext_own[24:28, :] = listed(6)
    ext_own[28:32, :] = listed(9)
    ext_left[0:8, :] = left2
    ext_left[8:16, :] = left
    ext_left[16:24, :] = own
    ext_left[24:28, :] = listed(5)
    ext_left[28:32, :] = listed(8)
    ext_right[0:8, :] = own
    ext_right[8:16, :] = right
    ext_right[16:24, :] = right2
    ext_right[24:28, :] = listed(7)
    ext_right[28:32, :] = listed(10)
    low = sub < 4
    below_ext = [full(5, 1), full(6, None), full(7, 2)]
    above_ext = [full(8, 1), full(9, None), full(10, 2)]
    for part in range(3):
        for b in range(8):
            ext_list[8 * part + b] = jnp.where(
                low,
                jnp.broadcast_to(below_ext[part][b : b + 1, :], (8, LANES)),
                jnp.broadcast_to(above_ext[part][b : b + 1, :], (8, LANES)),
            )
    own_listed = listed(0)
    tails = [(listed(11), own_listed), (own_listed, listed(17))]
    for part in range(2):
        for b in range(4):
            ext_list[24 + 4 * part + b] = jnp.where(
                low,
                jnp.broadcast_to(tails[part][0][b : b + 1, :], (8, LANES)),
                jnp.broadcast_to(tails[part][1][b : b + 1, :], (8, LANES)),
            )
    own_list = jnp.concatenate([listed(6), listed(9)], axis=0)
    new_own = banded_step(ext_own, stat_own, own, sub)
    new_left = banded_step(ext_left, stat_left, left, sub)
    new_right = banded_step(ext_right, stat_right, right, sub)
    new_list = listed_step(ext_list, stat_list, own_list)
    ext_own[0:8, :] = jnp.where(place[14], new_left, 0.0)
    ext_own[8:16, :] = new_own
    ext_own[16:24, :] = jnp.where(place[15], new_right, 0.0)
    ext_own[24:32, :] = new_list
    final = banded_step(ext_own, stat_own, new_own, sub)
    if last:
        out_ref[...] = final
        return
    ext_left[0:8, :] = final
    broadcast_heights(final, ext_left, sends, out)
    send_payload(out, out_ref, stored)


def stage(sources, depth, target, width, offset, level):
    levels = level.shape[0]
    for b in range(width // LANES):
        cols = slice(b * LANES, (b + 1) * LANES)
        where = pl.ds(offset + b * LANES, LANES)
        wet = (level < depth[ROW_DEPTH : ROW_DEPTH + 1, cols]).astype(jnp.float32)
        for c in range(2):
            value = sources[c][:, cols] * wet
            high = value.astype(jnp.bfloat16)
            low = (value - high.astype(jnp.float32)).astype(jnp.bfloat16)
            target[c * levels : (c + 1) * levels, where] = low
            target[(2 + c) * levels : (3 + c) * levels, where] = high
        target[4 * levels : 5 * levels, where] = wet.astype(jnp.bfloat16)


def weight_tile(line, index, highs, lows, base):
    high = jnp.zeros((TILE, TILE), jnp.bfloat16)
    low = jnp.zeros((TILE, TILE), jnp.bfloat16)
    for e in range(6):
        local = index[e] - base
        local = jnp.where(jnp.logical_and(local >= 0, local < TILE), local, -1)
        local = local.astype(jnp.float32).astype(jnp.bfloat16)
        hit = line == local
        high = jnp.where(hit, highs[e], high)
        low = jnp.where(hit, lows[e], low)
    return high, low


def weight_tiles(line, index, highs, lows, base, count):
    tiles = [weight_tile(line, index, highs, lows, base + n * TILE) for n in range(count)]
    return tuple(jnp.concatenate([tile[part] for tile in tiles], axis=0) for part in range(2))


def tile_line():
    line = lax.broadcasted_iota(jnp.int32, (TILE, TILE), 0)
    return line.astype(jnp.float32).astype(jnp.bfloat16)


def split_weights(rows, columns):
    weights = [rows[e : e + 1, columns] for e in range(6)]
    highs = [w.astype(jnp.bfloat16) for w in weights]
    lows = [(w - h.astype(jnp.float32)).astype(jnp.bfloat16) for w, h in zip(weights, highs)]
    return highs, lows


def product(rows, columns, high, low, levels):
    first = jnp.dot(rows[:, columns], high, preferred_element_type=jnp.float32)
    second = jnp.dot(rows[2 * levels :, columns], low, preferred_element_type=jnp.float32)
    return jnp.concatenate(
        [
            first[0 : 2 * levels] + first[2 * levels : 4 * levels] + second[0 : 2 * levels],
            first[4 * levels :] + second[2 * levels :],
        ],
        axis=0,
    )


def local_kernel(
    theta_in, salt_in, small, kappa_in, depth_in, pivots, part,
    theta, salt, kappa, depth8, kap, rows_own, loaded
):
    cells = small.shape[1]
    levels = pivots.shape[1] // 8
    arrivals = copies(
        [(depth_in, depth8), (kappa_in, kappa), (theta_in, theta), (salt_in, salt)], loaded
    )
    for copy in arrivals[:2]:
        copy.wait()
    for b in range(cells // LANES):
        cols = slice(b * LANES, (b + 1) * LANES)
        kap[pl.ds(b, levels - 1, stride=8), :] = kappa[:, cols]
    depth = depth8[...]
    before = jnp.zeros((8, LANES), jnp.float32)
    last_ratio = before
    for k in range(levels):
        rows = slice(8 * k, 8 * k + 8)
        if k < levels - 1:
            after = jnp.where(depth > k + 1, kap[rows, :], 0.0)
        else:
            after = jnp.zeros((8, LANES), jnp.float32)
        pivot = 1.0 + before + after - before * last_ratio
        inverse = 1.0 / pivot
        last_ratio = after * inverse
        pivots[0, rows, :] = last_ratio
        pivots[1, rows, :] = before * inverse
        pivots[2, rows, :] = inverse
        before = after
    index = [small[ROW_INDEX + e : ROW_INDEX + e + 1, :].astype(jnp.int32) for e in range(6)]
    weight = [small[ROW_WEIGHT + e : ROW_WEIGHT + e + 1, :] for e in range(6)]
    for e in range(5, 0, -1):
        taken = index[e] < 0
        for f in range(e):
            same = jnp.logical_and(index[e] == index[f], jnp.logical_not(taken))
            weight[f] = weight[f] + jnp.where(same, weight[e], 0.0)
            taken = jnp.logical_or(taken, same)
        index[e] = jnp.where(taken, -1, index[e])
    for e in range(6):
        part[PART_INDEX + e : PART_INDEX + e + 1, :] = index[e].astype(jnp.float32)
        part[PART_WEIGHT + e : PART_WEIGHT + e + 1, :] = weight[e]
    level = lax.broadcasted_iota(jnp.int32, (levels, LANES), 0).astype(jnp.float32)
    for copy in arrivals[2:]:
        copy.wait()
    stage((theta, salt), small, rows_own, cells, 0, level)
    line = tile_line()

    def block(t, carry):
        here = pl.ds(pl.multiple_of(t * TILE, TILE), TILE)
        idx = [part[PART_INDEX + e : PART_INDEX + e + 1, here].astype(jnp.int32) for e in range(6)]
        highs, lows = split_weights(part.at[pl.ds(PART_WEIGHT, 8), :], here)
        total = jnp.zeros((3 * levels, TILE), jnp.float32)
        for j in range(0, cells // TILE, 2):
            high, low = weight_tiles(line, idx, highs, lows, cells + j * TILE, 2)
            columns = slice(j * TILE, (j + 2) * TILE)
            total = total + product(rows_own, columns, high, low, levels)
        part[0 : 3 * levels, here] = total
        return carry

    lax.fori_loop(0, cells // TILE, block, 0)


def tracer_kernel(
    theta_in, salt_in, small, small_below, small_above, below, above, swap_in, swap_out, pivots, part,
    theta_out, salt_out, own, rows_ext, star, result, loaded, stored
):
    levels, cells = theta_out.shape
    listed = below.shape[1]
    arrivals = copies([(theta_in, own.at[0]), (salt_in, own.at[1])], loaded)
    level = lax.broadcasted_iota(jnp.int32, (levels, LANES), 0).astype(jnp.float32)
    odd = lax.axis_index("dom") % 2 == 1
    inner = pl.multiple_of(jnp.where(odd, 0, cells), LANES)
    outer = pl.multiple_of(jnp.where(odd, cells, 0), LANES)
    starts = (inner, outer, 2 * cells, 2 * cells + listed)
    depths = [source.at[pl.ds(2 * levels, SMALL), :] for source in (swap_in, swap_out)]
    depths += [small_below, small_above]
    for source, depth, start in zip((swap_in, swap_out, below, above), depths, starts):
        tracers = [source.at[pl.ds(c * levels, levels), :] for c in range(2)]
        stage(tracers, depth, rows_ext, source.shape[1], start, level)
    for copy in arrivals:
        copy.wait()
    line = tile_line()
    band = (TILE + cells) // TILE
    region = 2 * listed // TILE

    def block(t, carry):
        start = pl.multiple_of(t * TILE, TILE)
        here = pl.ds(start, TILE)
        idx = []
        for e in range(6):
            value = part[PART_INDEX + e : PART_INDEX + e + 1, here].astype(jnp.int32)
            outside = jnp.where(value >= 2 * cells, value - cells, -1)
            idx.append(jnp.where(value < cells, value, outside))
        highs, lows = split_weights(part.at[pl.ds(PART_WEIGHT, 8), :], here)
        total = part[0 : 3 * levels, here]
        spans = [(start + j * TILE, min(3, band - j)) for j in range(0, band, 3)]
        spans += [(2 * cells + j * TILE, min(2, region - j)) for j in range(0, region, 2)]
        for base, count in spans:
            base = pl.multiple_of(base, TILE)
            high, low = weight_tiles(line, idx, highs, lows, base, count)
            total = total + product(rows_ext, pl.ds(base, count * TILE), high, low, levels)
        for b in range(TILE // LANES):
            cols = slice(b * LANES, (b + 1) * LANES)
            sub = pl.ds(start + b * LANES, LANES)
            wet = level < small[ROW_DEPTH : ROW_DEPTH + 1, sub]
            for c in range(2):
                value = own[c, :, sub]
                change = total[c * levels : (c + 1) * levels, cols] - value * total[2 * levels :, cols]
                stepped = value + jnp.where(wet, change, 0.0)
                star[c, pl.ds(t * (TILE // LANES) + b, levels, stride=8), :] = stepped
        return carry

    lax.fori_loop(0, cells // TILE, block, 0)
    for c in range(2):
        star[c] = star[c] * pivots[2]
    before = [star[0, 0:8, :], star[1, 0:8, :]]
    for k in range(1, levels):
        rows = slice(8 * k, 8 * k + 8)
        factor = pivots[1, rows, :]
        for c in range(2):
            before[c] = star[c, rows, :] + factor * before[c]
            star[c, rows, :] = before[c]
    for k in range(levels - 2, -1, -1):
        rows = slice(8 * k, 8 * k + 8)
        factor = pivots[0, rows, :]
        for c in range(2):
            before[c] = star[c, rows, :] + factor * before[c]
            star[c, rows, :] = before[c]
    departures = []
    for c, out in enumerate((theta_out, salt_out)):
        for b in range(cells // LANES):
            cols = slice(b * LANES, (b + 1) * LANES)
            result[c, :, cols] = star[c, pl.ds(b, levels, stride=8), :]
            if b % 4 == 3:
                done = pl.ds((b - 3) * LANES, 4 * LANES)
                departures += copies(
                    [(result.at[c, :, done], out.at[:, done])],
                    stored.at[pl.ds(2 * c + b // 4, 1)],
                )
    for copy in departures:
        copy.wait()


HBM = pl.BlockSpec(memory_space=pltpu.HBM)
VMEM = pl.BlockSpec(memory_space=pltpu.VMEM)


def grant(mebibytes):
    return pltpu.CompilerParams(vmem_limit_bytes=mebibytes * 1024 * 1024)


def estimate(flops, size):
    return pl.CostEstimate(flops=flops, bytes_accessed=size, transcendentals=0)


def body(regions, doms, theta, salt, ssh, depth, neighbors, send_list, weights, kappa):
    levels, cells = theta.shape
    listed = send_list.shape[0]
    devices = regions * doms
    f32 = jnp.float32
    depth8 = depth.reshape(cells // LANES, LANES)
    ssh8 = ssh.reshape(cells // LANES, LANES)
    send4 = send_list.reshape(listed // LANES, LANES)
    def vmem(*shape, dtype=f32):
        return pltpu.VMEM(shape, dtype)

    def semaphores(count):
        return pltpu.SemaphoreType.DMA((count,))

    payload_shape = jax.ShapeDtypeStruct((devices, 3, 4, LANES), f32)

    def hbm(*arrays):
        return [pltpu.with_memory_space_constraint(array, pltpu.HBM) for array in arrays]

    payload, sends = pl.pallas_call(
        heights_kernel,
        out_shape=(payload_shape, jax.ShapeDtypeStruct((listed // LANES, LANES), jnp.int32)),
        in_specs=[HBM] * 2,
        out_specs=(HBM, VMEM),
        scratch_shapes=[vmem(8, LANES), vmem(*payload_shape.shape), semaphores(2 + PARALLEL)],
        compiler_params=grant(8),
        cost_estimate=estimate(1000, 1000),
        name="heights",
    )(*hbm(ssh8, send4))
    small, picked, picked_small, message = pl.pallas_call(
        pick_kernel,
        out_shape=(
            jax.ShapeDtypeStruct((SMALL, cells), f32),
            jax.ShapeDtypeStruct((2 * levels, listed), f32),
            jax.ShapeDtypeStruct((SMALL, listed), f32),
            jax.ShapeDtypeStruct((2 * levels + SMALL, cells), f32),
        ),
        in_specs=[HBM] * 7,
        out_specs=(VMEM,) * 3 + (HBM,),
        scratch_shapes=[
            vmem(levels, cells), vmem(levels, cells),
            vmem(8, LANES, dtype=jnp.int32), vmem(8, LANES), vmem(6, cells, dtype=jnp.int32),
            vmem(6, cells), vmem(listed // LANES, LANES, dtype=jnp.int32), semaphores(7), semaphores(3),
        ],
        compiler_params=grant(8),
        cost_estimate=estimate(2000000, 2000000),
        name="pick",
    )(*hbm(theta, salt, depth8, ssh8, neighbors, weights, send4))
    def device(i, j):
        return (i % regions) * doms + j

    inner = [(device(i, j), device(i, j ^ 1)) for i in range(regions) for j in range(doms)]
    outer = [
        (device(i, j), device(i, j + 1 if j % 2 else j - 1))
        for i in range(regions)
        for j in range(1, doms - 1)
    ]
    upward = [(device(i, j), device(i + 1, j)) for i in range(regions) for j in range(doms)]
    downward = [(target, source) for source, target in upward]
    below = lax.ppermute(picked, AXES, upward)
    above = lax.ppermute(picked, AXES, downward)
    small_below = lax.ppermute(picked_small, AXES, upward)
    small_above = lax.ppermute(picked_small, AXES, downward)
    swap_in = lax.ppermute(message, AXES, inner)
    swap_out = lax.ppermute(message, AXES, outer)
    heights = lax.all_to_all(payload, AXES, 0, 0)
    heights, small_later = lax.optimization_barrier((heights, small))
    pivots, part = pl.pallas_call(
        local_kernel,
        out_shape=(
            jax.ShapeDtypeStruct((3, 8 * levels, LANES), f32),
            jax.ShapeDtypeStruct((PART_WEIGHT + 8, cells), f32),
        ),
        in_specs=[HBM, HBM, VMEM, HBM, HBM],
        out_specs=(VMEM,) * 2,
        scratch_shapes=[
            vmem(levels, cells), vmem(levels, cells),
            vmem(levels - 1, cells), vmem(8, LANES, dtype=jnp.int32), vmem(8 * levels, LANES),
            vmem(5 * levels, cells, dtype=jnp.bfloat16), semaphores(4),
        ],
        compiler_params=grant(8),
        cost_estimate=estimate(40000000000, 4000000),
        name="local",
    )(*hbm(theta, salt), small_later, *hbm(kappa, depth8))
    small_below, small_above, swap_in, swap_out, heights, pivots, part = lax.optimization_barrier(
        (small_below, small_above, swap_in, swap_out, heights, pivots, part)
    )

    def subcycles(values, last):
        shape = jax.ShapeDtypeStruct((8, LANES), f32) if last else payload_shape
        return pl.pallas_call(
            functools.partial(surface_kernel, last=last, shape=(regions, doms)),
            out_shape=shape,
            in_specs=[VMEM] * 9,
            out_specs=VMEM if last else HBM,
            scratch_shapes=[vmem(8 * SMALL, LANES)] * 4
            + [vmem(32, LANES)] * 3
            + [vmem(32, 8, LANES), vmem(*shape.shape), semaphores(PARALLEL)],
            compiler_params=grant(8),
            cost_estimate=estimate(1000, 1000),
            name="surface_last" if last else "surface_first",
        )(
            small_below, small_above, values, small, swap_in, swap_out, sends, pivots, part
        )

    heights2 = lax.all_to_all(subcycles(heights, False), AXES, 0, 0)
    surface = subcycles(heights2, True)
    theta_next, salt_next = pl.pallas_call(
        tracer_kernel,
        out_shape=(jax.ShapeDtypeStruct((levels, cells), f32),) * 2,
        in_specs=[HBM] * 2 + [VMEM] * 9,
        out_specs=(HBM,) * 2,
        scratch_shapes=[
            vmem(2, levels, cells),
            vmem(5 * levels, 2 * cells + 2 * listed, dtype=jnp.bfloat16),
            vmem(2, 8 * levels, LANES), vmem(2, levels, cells), semaphores(2), semaphores(4),
        ],
        cost_estimate=estimate(4000000000, 8000000),
        compiler_params=grant(12),
        name="tracers",
    )(
        *hbm(theta, salt), small, small_below, small_above, below, above, swap_in, swap_out,
        pivots, part
    )
    return (theta_next, salt_next, surface.reshape(cells))


def solution(mesh):
    columns = P(None, AXES)
    cells = P(AXES)
    return jax.shard_map(
        functools.partial(body, mesh.shape["region"], mesh.shape["dom"]),
        mesh=mesh,
        in_specs=(columns, columns, cells, cells, columns, cells, columns, columns),
        out_specs=(columns, columns, cells),
        check_vma=False,
    )
```
